128 devices in a mesh: lat: 8 (over y_lo, z), lon: 16 (over y_hi, x, core).
Axes of the slice: x: 4, y: 4 (y_hi: 2, y_lo: 2; y = y_hi * 2 + y_lo), z: 4, core: 2. Of those that a mesh axis runs over, the one named last changes fastest.
Arguments:
- adjoint_field: float32 [128, 256, 4096], P(None, 'lat', 'lon'), may hold values from -6 to 6
- mixing_inverse: float32 [256, 128, 128], P('lat'), as said below
- cloud_top: int32 [256, 4096], P('lat', 'lon'), may hold values from 1 to 128
- conv_frac: float32 [256, 4096], P('lat', 'lon'), may hold values from 0.2 to 0.9
- thickness: float32 [128], replicated, may hold values from 0.3 to 3
- zonal_shift: int32 [128, 256], P(None, 'lat'), may hold values from 0 to 48
- zonal_frac: float32 [128, 256], P(None, 'lat'), may hold values from 0 to 1
- merid_courant: float32 [128, 256, 4096], P(None, 'lat', 'lon'), may hold values from 0.1 to 0.9
- obs_kernel: bfloat16 [262144, 128], P(('lat', 'lon')), may hold values from -6 to 6
- obs_depart: float32 [262144], P(('lat', 'lon')), may hold values from -6 to 6
- obs_dest: int32 [262144], P(('lat', 'lon')), may hold values from 0 to 127, as said below
- obs_col: int32 [262144], P(('lat', 'lon')), may hold values from 0 to 8191
- obs_count: int32 [128], P(('lat', 'lon')), may hold values from 16 to 2048, as said below
Outputs:
- adjoint_out: float32 [128, 256, 4096], P(None, 'lat', 'lon')
The draws below stay inside these ranges and needn't reach their ends.
Inputs may be any that keep to these rules, and one draw needn't show every extreme that they name: `obs_dest`: live rows of each device are in non-decreasing order of destination, at most 16 of them to one destination; some destination receives exactly 16 live rows from every device. Rows past a device's count carry no sounding. `obs_count`: some device has all its rows live. `mixing_inverse`: entries are positive.
All inputs are finite; a program needn't handle non-finite values.
Results may differ from the reference program's by a relative error of at most 0.00095.
Values may be sent and summed in bfloat16 or wider, within the bound.
A program may use at most 128 MiB of HBM per device.

```python
import math
import jax
import jax.numpy as jnp
from jax import lax

LEV = 128
RLAT = 32
CLON = 256
SHIFT_MAX = 48
CAP = 16
NLAT = 256
NLON = 4096
OBS_DEV = 2048
OBS = 262144
N_LAT = 8
N_LON = 16


def route_tables(key):
    devices = N_LAT * N_LON
    base = jax.random.fold_in(key, 7)
    key_counts, key_hot, key_full = jax.random.split(base, 3)
    counts = jax.random.randint(key_counts, (devices, devices), 0, CAP + 1)
    hot_dest = jax.random.randint(key_hot, (), 0, devices)
    full_source = jax.random.randint(key_full, (), 0, devices)
    device_ids = jnp.arange(devices)
    counts = jnp.where(device_ids[None, :] == hot_dest, CAP, counts)
    counts = jnp.where(device_ids[:, None] == full_source, CAP, counts)
    group_ends = jnp.cumsum(counts, axis=1)
    live_total = group_ends[:, -1]
    row_ids = jnp.arange(OBS_DEV)
    dest_ids = jnp.sum((row_ids[None, :, None] >= group_ends[:, None, :]).astype(jnp.int32), axis=2)
    dest_ids = jnp.where(row_ids[None, :] < live_total[:, None], dest_ids, 0)
    return (dest_ids.reshape(-1).astype(jnp.int32), live_total.astype(jnp.int32))


def draw_obs_dest(key, part):
    dest_ids, live_total = route_tables(key)
    return dest_ids


def draw_obs_count(key, part):
    dest_ids, live_total = route_tables(key)
    return live_total


def draw_zonal_shift(key, part):
    key_values, key_place = jax.random.split(jax.random.fold_in(key, 11))
    shifts = jax.random.randint(key_values, (LEV, NLAT), 0, SHIFT_MAX + 1)
    place = jax.random.randint(key_place, (), 0, LEV * NLAT)
    flat_ids = jnp.arange(LEV * NLAT).reshape(LEV, NLAT)
    return jnp.where(flat_ids == place, SHIFT_MAX, shifts).astype(jnp.int32)


def draw_mixing_inverse(key, part):
    rough = jax.random.uniform(jax.random.fold_in(key, 13), (NLAT, LEV, LEV), jnp.float32, 0.5, 1.5)
    level_ids = jnp.arange(LEV)
    distance = jnp.abs(level_ids[:, None] - level_ids[None, :]).astype(jnp.float32)
    reach = 8.0
    weight = 0.3
    spread = weight * jnp.exp(-distance / reach)[None] * rough
    return jnp.where(distance[None] == 0.0, 0.6 + 0.4 * rough, spread).astype(jnp.float32)


def set_ends(result, own_key, smallest, high):
    shape = result.shape
    spot = [jax.random.randint(jax.random.fold_in(own_key, axis), (), 0, shape[axis]) for axis in range(len(shape))]
    result = result.at[tuple(spot)].set(smallest)
    longest = shape.index(max(shape))
    spot[longest] = (spot[longest] + 1) % shape[longest]
    return result.at[tuple(spot)].set(high)


def steps_of(own_key, dims, shards, least, top_value):
    gain, own = 1.0, jax.random.fold_in(own_key, 6)
    for position, parts in shards:
        steps = jnp.exp(jax.random.uniform(jax.random.fold_in(own, position), (parts,), jnp.float32, least / len(shards), top_value / len(shards)))
        gain = gain * jnp.repeat(steps, dims[position] // parts).reshape([-1 if axis == position else 1 for axis in range(len(dims))])
    return gain


def centred(key, dims, width, limit, pieces=(), kind=jnp.bfloat16):
    drawn = jax.random.normal(key, dims, jnp.float32) * width
    if len(pieces) > 0:
        drawn = steps_of(key, dims, pieces, -0.22, 0.18) * drawn
    return jnp.clip(drawn, min=-limit, max=limit).astype(kind)


def setup_inputs(seed: int = 0) -> dict:
    seeds = jax.random.split(jax.random.key(seed), 14)
    adjoint_field = centred(seeds[0], (LEV, NLAT, NLON), 1.0, 6.0, ((1, 8), (2, 16)), jnp.float32)
    mixing_inverse = draw_mixing_inverse(jax.random.fold_in(seeds[13], 71), 0)
    cloud_top = set_ends(jax.random.randint(seeds[2], (NLAT, NLON), 1, LEV + 1), jax.random.fold_in(seeds[2], 1), 1, LEV).astype(jnp.int32)
    conv_frac = jnp.clip(0.2 + 0.7 * jax.random.uniform(seeds[3], (NLAT, NLON), jnp.float32) ** steps_of(seeds[3], (NLAT, NLON), ((0, 8), (1, 16)), -0.2, 0.2), 0.2, 0.9)
    thickness = jnp.clip(jnp.exp(jax.random.uniform(seeds[4], (LEV,), jnp.float32, math.log(0.3), math.log(3.0))), 0.3, 3.0)
    zonal_shift = draw_zonal_shift(jax.random.fold_in(seeds[13], 71), 0)
    zonal_frac = jnp.clip(1.0 * jax.random.uniform(seeds[6], (LEV, NLAT), jnp.float32) ** steps_of(seeds[6], (LEV, NLAT), ((1, 8),), -0.2, 0.2), 0.0, 1.0)
    merid_courant = jnp.clip(0.1 + 0.79999997 * jax.random.uniform(seeds[7], (LEV, NLAT, NLON), jnp.float32) ** steps_of(seeds[7], (LEV, NLAT, NLON), ((1, 8), (2, 16)), -0.2, 0.2), 0.1, 0.9)
    obs_kernel = centred(seeds[8], (OBS, LEV), 1.0, 6.0, ((0, 128),))
    obs_depart = centred(seeds[9], (OBS,), 1.0, 6.0, ((0, 128),), jnp.float32)
    obs_dest = draw_obs_dest(jax.random.fold_in(seeds[13], 71), 0)
    obs_col = set_ends(jax.random.randint(seeds[11], (OBS,), 0, RLAT * CLON), jax.random.fold_in(seeds[11], 1), 0, (RLAT * CLON) - 1).astype(jnp.int32)
    obs_count = draw_obs_count(jax.random.fold_in(seeds[13], 71), 0)
    return dict(adjoint_field=adjoint_field, mixing_inverse=mixing_inverse, cloud_top=cloud_top, conv_frac=conv_frac, thickness=thickness, zonal_shift=zonal_shift, zonal_frac=zonal_frac, merid_courant=merid_courant, obs_kernel=obs_kernel, obs_depart=obs_depart, obs_dest=obs_dest, obs_col=obs_col, obs_count=obs_count)


def reference(adjoint_field, mixing_inverse, cloud_top, conv_frac, thickness, zonal_shift, zonal_frac, merid_courant, obs_kernel, obs_depart, obs_dest, obs_col, obs_count):
    row_ids = jnp.arange(OBS, dtype=jnp.int32)
    owner_ids = row_ids // OBS_DEV
    live_rows = (row_ids % OBS_DEV) < obs_count[owner_ids]
    contribution = jnp.where(live_rows[:, None], obs_kernel.astype(jnp.float32) * obs_depart[:, None], 0.0).astype(jnp.bfloat16)
    lat_index = obs_dest // N_LON
    lon_index = obs_dest % N_LON
    global_row = lat_index * RLAT + obs_col // CLON
    global_col = lon_index * CLON + obs_col % CLON
    cell_ids = (global_row * NLON + global_col).astype(jnp.int32)
    forcing = jax.ops.segment_sum(contribution.astype(jnp.float32), cell_ids, num_segments=NLAT * NLON)
    field_forced = adjoint_field + forcing.T.reshape(LEV, NLAT, NLON)
    field_mixed = jnp.einsum("rkj,jrc->krc", mixing_inverse, field_forced, precision=lax.Precision.HIGHEST)
    level_ids = jnp.arange(LEV, dtype=jnp.int32)[:, None, None]
    in_cloud = (level_ids < cloud_top[None, :, :]).astype(jnp.float32)
    layer_mass = thickness[:, None, None]
    cloud_total = jnp.sum(in_cloud * field_mixed, axis=0)
    cloud_mass = jnp.sum(in_cloud * layer_mass, axis=0)
    field_convected = field_mixed + conv_frac[None] * in_cloud * (layer_mass * (cloud_total / cloud_mass)[None] - field_mixed)
    col_ids = jnp.arange(NLON, dtype=jnp.int32)[None, None, :]
    first_index = (col_ids + zonal_shift[:, :, None]) % NLON
    second_index = (first_index + 1) % NLON
    first_cells = jnp.take_along_axis(field_convected, first_index, axis=2)
    second_cells = jnp.take_along_axis(field_convected, second_index, axis=2)
    fraction = zonal_frac[:, :, None]
    field_zonal = (1.0 - fraction) * first_cells + fraction * second_cells
    zero_row = jnp.zeros((LEV, 1, NLON), jnp.float32)
    next_field = jnp.concatenate([field_zonal[:, 1:], zero_row], axis=1)
    next_courant = jnp.concatenate([merid_courant[:, 1:], zero_row], axis=1)
    return (1.0 - merid_courant) * field_zonal + next_courant * next_field
```

```python
import functools

import jax
import jax.numpy as jnp
from jax import lax
from jax.experimental import pallas as pl
from jax.experimental.pallas import tpu as pltpu
from jax.sharding import PartitionSpec as P

MESH = pl.DeviceIdType.MESH
F32 = jnp.float32
BF16 = jnp.bfloat16
I32 = jnp.int32
DMA = pltpu.SemaphoreType.DMA
NLAT, NLON, NDEV = 8, 16, 128
LEV, ROWS, COLS = 128, 32, 256
OBS, CAP = 2048, 16
PACK = 64


def iota(shape, axis):
    return lax.broadcasted_iota(I32, shape, axis)


def exchange_kernel(
    count_ref, kernel_ref, depart_ref, dest_ref, col_ref, rows_out, meta_out,
    send_rows, send_meta, contribution, entered, sems,
):
    lat, lon = lax.axis_index("lat"), lax.axis_index("lon")
    me = lat * NLON + lon
    barrier = pltpu.get_barrier_semaphore()

    def greet(target_of, semaphore, count):
        def body(step, carry):
            pl.semaphore_signal(semaphore, inc=1, device_id=target_of(step), device_id_type=MESH)
            return carry

        lax.fori_loop(1, count, body, 0)

    lon_peer = lambda step: (lat, lax.rem(lon + step, NLON))
    lat_peer = lambda step: (lax.rem(lat + step, NLAT), lon)
    greet(lon_peer, barrier, NLON)
    greet(lat_peer, barrier, NLAT)

    dest = dest_ref[...]
    sub, lane = iota((16, 128), 0), iota((16, 128), 1)
    flat = sub * 128 + lane
    rank = jnp.zeros((16, 128), I32)
    for step in range(1, CAP):
        rolled = pltpu.roll(dest, step, 1)
        before = jnp.where(lane < step, pltpu.roll(rolled, 1, 0), rolled)
        rank = rank + jnp.where((before == dest) & (flat >= step), 1, 0)
    live = flat < count_ref[0]
    slot = jnp.where(live, dest * CAP + rank, -1)
    dest_live = jnp.where(live, dest, -1)
    cells = col_ref[...]
    cell_row = (cells // COLS).astype(F32)
    cell_col = (cells % COLS).astype(F32)

    depart_t = jnp.transpose(depart_ref[...])
    for block in range(16):
        span = pl.ds(block * 128, 128)
        contribution[span, :] = (
            kernel_ref[span, :].astype(F32) * jnp.broadcast_to(depart_t[:, block : block + 1], (128, 128))
        ).astype(BF16)

    pl.semaphore_wait(barrier, NLON + NLAT - 2)
    greet(lat_peer, entered, NLAT)

    big_sub = iota((128, 128), 0)
    mine = (big_sub // CAP) == lax.rem(me, 8)
    meta = jnp.zeros((128, 128), F32)
    nt = (((1,), (1,)), ((), ()))
    for block in range(16):
        owner = jnp.where(dest_live[block : block + 1, :] == big_sub, 1.0, 0.0).astype(BF16)
        place = (rank[block : block + 1, :] == big_sub % CAP) & mine
        row_part = jnp.where(place, cell_row[block : block + 1, :], 0.0).astype(BF16)
        col_part = jnp.where(place, cell_col[block : block + 1, :], 0.0).astype(BF16)
        meta = meta + float(COLS) * lax.dot_general(owner, row_part, nt, preferred_element_type=F32)
        meta = meta + lax.dot_general(owner, col_part, nt, preferred_element_type=F32)
    meta = meta.astype(I32)
    for dst in range(NDEV):
        send_meta[dst, :, :] = meta[dst : dst + 1, :]

    for out_block in range(16):
        total = jnp.zeros((128, 128), F32)
        for block in range(out_block + 1):
            hit = jnp.where(slot[block : block + 1, :] == big_sub + out_block * 128, 1.0, 0.0).astype(BF16)
            total = total + jnp.dot(
                hit, contribution[pl.ds(block * 128, 128), :], preferred_element_type=F32
            )
        send_rows[pl.ds(out_block * 8, 8), :, :] = total.astype(BF16).reshape(8, CAP, LEV)

    pl.semaphore_wait(entered, NLAT - 1)

    def send(step, carry):
        target = lax.rem(me + step, NDEV)
        where = (target // NLON, lax.rem(target, NLON))
        pltpu.make_async_remote_copy(
            send_rows.at[target], rows_out.at[me], sems.at[0], sems.at[1],
            device_id=where, device_id_type=MESH,
        ).start()
        pltpu.make_async_remote_copy(
            send_meta.at[target], meta_out.at[me], sems.at[2], sems.at[3],
            device_id=where, device_id_type=MESH,
        ).start()
        return carry

    lax.fori_loop(1, NDEV, send, 0)
    own_rows = pltpu.make_async_copy(send_rows.at[me], rows_out.at[me], sems.at[4])
    own_meta = pltpu.make_async_copy(send_meta.at[me], meta_out.at[me], sems.at[5])
    own_rows.start()
    own_meta.start()
    own_rows.wait()
    own_meta.wait()
    others = pl.ds(0, NDEV - 1)
    pltpu.make_async_copy(send_rows.at[others], send_rows.at[others], sems.at[0]).wait()
    pltpu.make_async_copy(send_meta.at[others], send_meta.at[others], sems.at[2]).wait()
    pltpu.make_async_copy(rows_out.at[others], rows_out.at[others], sems.at[1]).wait()
    pltpu.make_async_copy(meta_out.at[others], meta_out.at[others], sems.at[3]).wait()


def exchange(obs_count, obs_kernel, obs_depart, obs_dest, obs_col):
    vmem = pl.BlockSpec(memory_space=pltpu.VMEM)
    return pl.pallas_call(
        exchange_kernel,
        out_shape=[
            jax.ShapeDtypeStruct((NDEV, CAP, LEV), BF16),
            jax.ShapeDtypeStruct((NDEV, 1, 128), I32),
        ],
        in_specs=[pl.BlockSpec(memory_space=pltpu.SMEM)] + [vmem] * 4,
        out_specs=[vmem, vmem],
        scratch_shapes=[
            pltpu.VMEM((NDEV, CAP, LEV), BF16),
            pltpu.VMEM((NDEV, 1, 128), I32),
            pltpu.VMEM((OBS, LEV), BF16),
            pltpu.SemaphoreType.REGULAR,
            DMA((6,)),
        ],
        compiler_params=pltpu.CompilerParams(collective_id=0, has_side_effects=True),
        name="exchange",
    )(
        obs_count, obs_kernel, obs_depart.reshape(16, 128),
        obs_dest.reshape(16, 128), obs_col.reshape(16, 128),
    )


def column_kernel(
    rows_ref, meta_ref, field_ref, mixing_ref, top_ref, frac_ref, thick_ref,
    out_ref, halo_ref, rows_t, cols_hot, row_of, thick_full, masked, forced,
):
    step = pl.program_id(0)

    @pl.when(step == 0)
    def _():
        cells = jnp.sum(meta_ref[...].reshape(16, 8, 128), axis=1)
        row_of[...] = jnp.concatenate(
            [(cells[b : b + 1, :] // COLS) for b in range(16)], axis=1
        ).astype(F32)
        columns = jnp.transpose((cells % COLS).astype(F32))
        eye = jnp.where(iota((128, 128), 0) == iota((128, 128), 1), 1.0, 0.0).astype(BF16)
        wide = iota((128, COLS), 1).astype(F32)
        for b in range(16):
            span = pl.ds(b * 128, 128)
            cols_hot[span, :] = jnp.where(
                jnp.broadcast_to(columns[:, b : b + 1], (128, COLS)) == wide, 1.0, 0.0
            ).astype(BF16)
            rows_t[:, span] = lax.dot_general(
                eye, rows_ref[span, :], (((1,), (1,)), ((), ())), preferred_element_type=F32
            ).astype(BF16)
        thick = jnp.transpose(jnp.broadcast_to(thick_ref[...], (128, 128)))
        thick_full[:, 0:128] = thick
        thick_full[:, 128:256] = thick

    base = (step * 8).astype(F32)
    row_ids = row_of[...]
    for r in range(8):
        mask = jnp.where(row_ids == base + float(r), 1.0, 0.0).astype(BF16)
        masked[pl.ds(r * 128, 128), :] = rows_t[...] * mask
    forced[...] = jnp.dot(masked[...], cols_hot[...], preferred_element_type=F32)
    levels = iota((LEV, COLS), 0)
    flat_field = field_ref.reshape(2048, 128)

    def row(r, carry):
        adjoint = jnp.concatenate(
            [flat_field[pl.ds(r, 128, stride=16), :], flat_field[pl.ds(8 + r, 128, stride=16), :]], axis=1
        )
        start = pl.multiple_of(r * 128, 128)
        value = adjoint + forced[pl.ds(start, 128), :]
        matrix = mixing_ref[r]
        v_hi = value.astype(BF16)
        v_lo = (value - v_hi.astype(F32)).astype(BF16)
        m_hi = matrix.astype(BF16)
        m_lo = (matrix - m_hi.astype(F32)).astype(BF16)
        mixed = (
            jnp.dot(m_hi, v_lo, preferred_element_type=F32)
            + jnp.dot(m_lo, v_hi, preferred_element_type=F32)
        ) + jnp.dot(m_hi, v_hi, preferred_element_type=F32)
        cloudy = levels < top_ref[pl.ds(r, 1), :]
        thick = thick_full[...]
        total = jnp.sum(jnp.where(cloudy, mixed, 0.0), axis=0, keepdims=True)
        mass = jnp.sum(jnp.where(cloudy, thick, 0.0), axis=0, keepdims=True)
        fraction = frac_ref[pl.ds(r, 1), :]
        convected = jnp.where(cloudy, mixed + fraction * (thick * (total / mass) - mixed), mixed)
        out_ref[r] = convected
        low = convected[0:64, 0:128]
        high = pltpu.roll(convected[64:128, 0:128], PACK, 1)
        halo_ref[r] = jnp.where(iota((64, 128), 1) < PACK, low, high)
        return carry

    lax.fori_loop(0, 8, row, 0)


def column_step(rows, meta, field, mixing, top, frac, thick):
    whole = lambda *shape: pl.BlockSpec(shape, lambda i: (0,) * len(shape))
    return pl.pallas_call(
        column_kernel,
        grid=(4,),
        out_shape=[
            jax.ShapeDtypeStruct((ROWS, LEV, COLS), F32),
            jax.ShapeDtypeStruct((ROWS, 64, 128), F32),
        ],
        in_specs=[
            whole(OBS, LEV),
            whole(NDEV, 128),
            pl.BlockSpec((LEV, 1, 16, 128), lambda i: (0, i, 0, 0)),
            pl.BlockSpec((8, LEV, LEV), lambda i: (i, 0, 0)),
            pl.BlockSpec((8, COLS), lambda i: (i, 0)),
            pl.BlockSpec((8, COLS), lambda i: (i, 0)),
            whole(1, LEV),
        ],
        out_specs=[
            pl.BlockSpec((8, LEV, COLS), lambda i: (i, 0, 0)),
            pl.BlockSpec((8, 64, 128), lambda i: (i, 0, 0)),
        ],
        scratch_shapes=[
            pltpu.VMEM((LEV, OBS), BF16),
            pltpu.VMEM((OBS, COLS), BF16),
            pltpu.VMEM((1, OBS), F32),
            pltpu.VMEM((LEV, COLS), F32),
            pltpu.VMEM((8 * LEV, OBS), BF16),
            pltpu.VMEM((8 * LEV, COLS), F32),
        ],
        compiler_params=pltpu.CompilerParams(vmem_limit_bytes=56 * 1024 * 1024),
        name="column",
    )(rows, meta, field, mixing, top, frac, thick)


def transport_kernel(
    conv_ref, halo_ref, next_conv_ref, next_halo_ref, next_shift_ref, next_frac_ref, next_courant_ref,
    shift_ref, frac_ref, courant_ref, out_ref, shift_pad, frac_pad, carried,
):
    step = pl.program_id(0)
    lane = iota((LEV, 128), 1)
    tail = jnp.where(iota((LEV, 128), 0) < 64, 0, PACK)

    def zonal(first, second, packed, shift, fraction):
        def pick(offset):
            index = lane + offset
            inside = index < 128
            wrapped = index & 127
            a = jnp.take_along_axis(first, wrapped, axis=1)
            b = jnp.take_along_axis(second, wrapped, axis=1)
            c = jnp.take_along_axis(packed, (wrapped + tail) & 127, axis=1)
            return jnp.where(inside, a, b), jnp.where(inside, b, c)

        left, right = pick(shift)
        left_next, right_next = pick(shift + 1)
        keep = 1.0 - fraction
        return keep * left + fraction * left_next, keep * right + fraction * right_next

    def doubled(packed):
        return jnp.concatenate([packed, packed], axis=0)

    @pl.when(step == 0)
    def _():
        shift_pad[...] = jnp.concatenate([shift_ref[...], jnp.zeros((LEV, 96), I32)], axis=1)
        frac_pad[...] = jnp.concatenate([frac_ref[...], jnp.zeros((LEV, 96), F32)], axis=1)
        last = lax.axis_index("lat") == NLAT - 1
        shift = jnp.transpose(jnp.broadcast_to(next_shift_ref[...], (128, 128)))
        fraction = jnp.transpose(jnp.broadcast_to(next_frac_ref[...], (128, 128)))
        left, right = zonal(
            next_conv_ref[:, 0:128], next_conv_ref[:, 128:256], doubled(next_halo_ref[...]), shift, fraction
        )
        carried[:, 0:128] = jnp.where(last, 0.0, next_courant_ref[:, 0:128] * left)
        carried[:, 128:256] = jnp.where(last, 0.0, next_courant_ref[:, 128:256] * right)

    flat_courant = courant_ref.reshape(2048, 128)
    flat_out = out_ref.reshape(2048, 128)
    first_row = (3 - step) * 8

    def row(back, carry):
        r = 7 - back
        here = jnp.full((LEV, 128), first_row + r, I32)
        shift = jnp.take_along_axis(shift_pad[...], here, axis=1)
        fraction = jnp.take_along_axis(frac_pad[...], here, axis=1)
        parts = zonal(
            conv_ref[r, :, 0:128], conv_ref[r, :, 128:256], doubled(halo_ref[r]), shift, fraction
        )
        for half in range(2):
            at = pl.ds(half * 8 + r, 128, stride=16)
            span = pl.ds(half * 128, 128)
            moved = flat_courant[at, :] * parts[half]
            flat_out[at, :] = parts[half] - moved + carried[:, span]
            carried[:, span] = moved
        return carry

    lax.fori_loop(0, 8, row, 0)


def transport(conv, halo, next_conv, next_halo, next_shift, next_frac, next_courant, shift, frac, courant):
    whole = lambda *shape: pl.BlockSpec(shape, lambda i: (0,) * len(shape))
    blocked = pl.BlockSpec((LEV, 1, 16, 128), lambda i: (0, 3 - i, 0, 0))
    return pl.pallas_call(
        transport_kernel,
        grid=(4,),
        out_shape=jax.ShapeDtypeStruct((LEV, 4, 16, 128), F32),
        in_specs=[
            pl.BlockSpec((8, LEV, COLS), lambda i: (3 - i, 0, 0)),
            pl.BlockSpec((8, 64, 128), lambda i: (3 - i, 0, 0)),
            whole(LEV, COLS),
            whole(64, 128),
            whole(1, LEV),
            whole(1, LEV),
            whole(LEV, COLS),
            whole(LEV, ROWS),
            whole(LEV, ROWS),
            blocked,
        ],
        out_specs=blocked,
        scratch_shapes=[
            pltpu.VMEM((LEV, 128), I32),
            pltpu.VMEM((LEV, 128), F32),
            pltpu.VMEM((LEV, COLS), F32),
        ],
        compiler_params=pltpu.CompilerParams(vmem_limit_bytes=40 * 1024 * 1024),
        name="transport",
    )(conv, halo, next_conv, next_halo, next_shift, next_frac, next_courant, shift, frac, courant)


def tiles(value):
    return value.reshape(LEV, 4, 8, 2, 128).transpose(0, 1, 3, 2, 4).reshape(LEV, 4, 16, 128)


def untiles(value):
    return value.reshape(LEV, 4, 2, 8, 128).transpose(0, 1, 3, 2, 4).reshape(LEV, ROWS, COLS)


def shards(
    adjoint_field, mixing_inverse, cloud_top, conv_frac, thickness, zonal_shift, zonal_frac,
    merid_courant, obs_kernel, obs_depart, obs_dest, obs_col, obs_count,
):
    lat_pairs = [(i + 1, i) for i in range(NLAT - 1)]
    lon_pairs = [((i + 1) % NLON, i) for i in range(NLON)]
    from_lat = lambda value: lax.ppermute(value, "lat", lat_pairs)
    from_lon = lambda value: lax.ppermute(value, "lon", lon_pairs)
    next_courant = from_lat(merid_courant[:, 0, :])
    next_shift = from_lat(zonal_shift[:, 0].reshape(1, LEV))
    next_frac = from_lat(zonal_frac[:, 0].reshape(1, LEV))
    rows, meta = exchange(obs_count, obs_kernel, obs_depart, obs_dest, obs_col)
    conv, edge = column_step(
        rows.reshape(OBS, LEV), meta.reshape(NDEV, 128), tiles(adjoint_field), mixing_inverse,
        cloud_top, conv_frac, thickness.reshape(1, LEV),
    )
    halo = from_lon(edge)
    next_conv = from_lat(conv[0])
    next_halo = from_lat(halo[0])
    out = transport(
        conv, halo, next_conv, next_halo, next_shift, next_frac, next_courant,
        zonal_shift, zonal_frac, tiles(merid_courant),
    )
    return untiles(out)


def solution(mesh):
    split = P(None, "lat", "lon")
    both = P(("lat", "lon"))
    return jax.shard_map(
        shards,
        mesh=mesh,
        in_specs=(
            split, P("lat", None, None), P("lat", "lon"), P("lat", "lon"), P(), P(None, "lat"), P(None, "lat"),
            split, P(("lat", "lon"), None), both, both, both, both,
        ),
        out_specs=split,
        check_vma=False,
    )
```

```python
import functools

import jax
import jax.numpy as jnp
from jax import lax
from jax.experimental import pallas as pl
from jax.experimental.pallas import tpu as pltpu
from jax.sharding import PartitionSpec as P

MESH = pl.DeviceIdType.MESH
F32 = jnp.float32
BF16 = jnp.bfloat16
I32 = jnp.int32
DMA = pltpu.SemaphoreType.DMA
NLAT, NLON, NDEV = 8, 16, 128
LEV, ROWS, COLS = 128, 32, 256
OBS, CAP = 2048, 16
PACK = 64
SHIFT_MAX = 48


def iota(shape, axis):
    return lax.broadcasted_iota(I32, shape, axis)


def exchange_kernel(
    count_ref, kernel_ref, depart_ref, dest_ref, col_ref, rows_out, meta_out,
    send_rows, send_meta, contribution, entered, sems,
):
    lat, lon = lax.axis_index("lat"), lax.axis_index("lon")
    me = lat * NLON + lon
    barrier = pltpu.get_barrier_semaphore()

    def greet(target_of, semaphore, count):
        def body(step, carry):
            pl.semaphore_signal(semaphore, inc=1, device_id=target_of(step), device_id_type=MESH)
            return carry

        lax.fori_loop(1, count, body, 0)

    lon_peer = lambda step: (lat, lax.rem(lon + step, NLON))
    lat_peer = lambda step: (lax.rem(lat + step, NLAT), lon)
    greet(lon_peer, barrier, NLON)
    greet(lat_peer, barrier, NLAT)

    dest = dest_ref[...]
    sub, lane = iota((16, 128), 0), iota((16, 128), 1)
    flat = sub * 128 + lane
    rank = jnp.zeros((16, 128), I32)
    for step in range(1, CAP):
        rolled = pltpu.roll(dest, step, 1)
        before = jnp.where(lane < step, pltpu.roll(rolled, 1, 0), rolled)
        rank = rank + jnp.where((before == dest) & (flat >= step), 1, 0)
    live = flat < count_ref[0]
    slot = jnp.where(live, dest * CAP + rank, -1)
    dest_live = jnp.where(live, dest, -1)
    cells = col_ref[...]
    cell_row = (cells // COLS).astype(F32)
    cell_col = (cells % COLS).astype(F32)

    depart_t = jnp.transpose(depart_ref[...])
    for block in range(16):
        span = pl.ds(block * 128, 128)
        contribution[span, :] = (
            kernel_ref[span, :].astype(F32) * jnp.broadcast_to(depart_t[:, block : block + 1], (128, 128))
        ).astype(BF16)

    pl.semaphore_wait(barrier, NLON + NLAT - 2)
    greet(lat_peer, entered, NLAT)

    big_sub = iota((128, 128), 0)
    mine = (big_sub // CAP) == lax.rem(me, 8)
    meta = jnp.zeros((128, 128), F32)
    nt = (((1,), (1,)), ((), ()))
    for block in range(16):
        owner = jnp.where(dest_live[block : block + 1, :] == big_sub, 1.0, 0.0).astype(BF16)
        place = (rank[block : block + 1, :] == big_sub % CAP) & mine
        row_part = jnp.where(place, cell_row[block : block + 1, :], 0.0).astype(BF16)
        col_part = jnp.where(place, cell_col[block : block + 1, :], 0.0).astype(BF16)
        meta = meta + float(COLS) * lax.dot_general(owner, row_part, nt, preferred_element_type=F32)
        meta = meta + lax.dot_general(owner, col_part, nt, preferred_element_type=F32)
    meta = meta.astype(I32)
    for dst in range(NDEV):
        send_meta[dst, :, :] = meta[dst : dst + 1, :]

    for out_block in range(16):
        total = jnp.zeros((128, 128), F32)
        for block in range(out_block + 1):
            hit = jnp.where(slot[block : block + 1, :] == big_sub + out_block * 128, 1.0, 0.0).astype(BF16)
            total = total + jnp.dot(
                hit, contribution[pl.ds(block * 128, 128), :], preferred_element_type=F32
            )
        send_rows[pl.ds(out_block * 8, 8), :, :] = total.astype(BF16).reshape(8, CAP, LEV)

    pl.semaphore_wait(entered, NLAT - 1)

    def send(step, carry):
        target = lax.rem(me + step, NDEV)
        where = (target // NLON, lax.rem(target, NLON))
        pltpu.make_async_remote_copy(
            send_rows.at[target], rows_out.at[me], sems.at[0], sems.at[1],
            device_id=where, device_id_type=MESH,
        ).start()
        pltpu.make_async_remote_copy(
            send_meta.at[target], meta_out.at[me], sems.at[2], sems.at[3],
            device_id=where, device_id_type=MESH,
        ).start()
        return carry

    lax.fori_loop(1, NDEV, send, 0)
    own_rows = pltpu.make_async_copy(send_rows.at[me], rows_out.at[me], sems.at[4])
    own_meta = pltpu.make_async_copy(send_meta.at[me], meta_out.at[me], sems.at[5])
    own_rows.start()
    own_meta.start()
    own_rows.wait()
    own_meta.wait()
    others = pl.ds(0, NDEV - 1)
    pltpu.make_async_copy(send_rows.at[others], send_rows.at[others], sems.at[0]).wait()
    pltpu.make_async_copy(send_meta.at[others], send_meta.at[others], sems.at[2]).wait()
    pltpu.make_async_copy(rows_out.at[others], rows_out.at[others], sems.at[1]).wait()
    pltpu.make_async_copy(meta_out.at[others], meta_out.at[others], sems.at[3]).wait()


def exchange(obs_count, obs_kernel, obs_depart, obs_dest, obs_col):
    vmem = pl.BlockSpec(memory_space=pltpu.VMEM)
    return pl.pallas_call(
        exchange_kernel,
        out_shape=[
            jax.ShapeDtypeStruct((NDEV, CAP, LEV), BF16),
            jax.ShapeDtypeStruct((NDEV, 1, 128), I32),
        ],
        in_specs=[pl.BlockSpec(memory_space=pltpu.SMEM)] + [vmem] * 4,
        out_specs=[vmem, vmem],
        scratch_shapes=[
            pltpu.VMEM((NDEV, CAP, LEV), BF16),
            pltpu.VMEM((NDEV, 1, 128), I32),
            pltpu.VMEM((OBS, LEV), BF16),
            pltpu.SemaphoreType.REGULAR,
            DMA((6,)),
        ],
        compiler_params=pltpu.CompilerParams(collective_id=0, has_side_effects=True),
        name="exchange",
    )(
        obs_count, obs_kernel, obs_depart.reshape(16, 128),
        obs_dest.reshape(16, 128), obs_col.reshape(16, 128),
    )


def column_kernel(
    rows_ref, meta_ref, field_ref, mixing_ref, top_ref, frac_ref, thick_ref, courant_ref, shift_ref, zfrac_ref,
    out_ref, halo_in, next_in, next_halo_in, next_given_in,
    rows_t, cols_hot, row_of, thick_full, masked, forced, given, first, edge, halo_sems, next_sems,
):
    step = pl.program_id(0)
    lat, lon = lax.axis_index("lat"), lax.axis_index("lon")
    west = lax.rem(lon + NLON - 1, NLON)
    east = lax.rem(lon + 1, NLON)
    north = lax.rem(lat + NLAT - 1, NLAT)
    has_north, has_south = lat > 0, lat < NLAT - 1

    def halo_copy(block):
        return pltpu.make_async_remote_copy(
            edge.at[pl.ds(block * 8, 8)], halo_in.at[pl.ds(block * 8, 8)],
            halo_sems.at[0, block], halo_sems.at[1, block], device_id=(lat, west), device_id_type=MESH,
        )

    def next_copy(which):
        source = (given, first, edge.at[0])[which]
        target = (next_given_in, next_in, next_halo_in)[which]
        column = (lon, lon, west)[which]
        return pltpu.make_async_remote_copy(
            source, target, next_sems.at[0, which], next_sems.at[1, which],
            device_id=(north, column), device_id_type=MESH,
        )

    @pl.when(step == 0)
    def _():
        barrier = pltpu.get_barrier_semaphore()
        south = lax.rem(lat + 1, NLAT)
        for target in (
            (lat, west), (lat, east), (north, lon), (south, lon), (north, west), (south, east)
        ):
            pl.semaphore_signal(barrier, inc=1, device_id=target, device_id_type=MESH)
        flat_courant = courant_ref.reshape(2048, 128)
        given[:, 0:128] = flat_courant[pl.ds(0, 128, stride=16), :]
        given[:, 128:256] = flat_courant[pl.ds(8, 128, stride=16), :]
        first_shift = jnp.broadcast_to(shift_ref[0:1, :].astype(F32), (128, 128))
        given[:, 256:384] = jnp.transpose(first_shift)
        given[:, 384:512] = jnp.transpose(jnp.broadcast_to(zfrac_ref[0:1, :], (128, 128)))
        cells = jnp.sum(meta_ref[...].reshape(16, 8, 128), axis=1)
        row_of[...] = jnp.concatenate(
            [(cells[b : b + 1, :] // COLS) for b in range(16)], axis=1
        ).astype(F32)
        columns = jnp.transpose((cells % COLS).astype(F32))
        eye = jnp.where(iota((128, 128), 0) == iota((128, 128), 1), 1.0, 0.0).astype(BF16)
        wide = iota((128, COLS), 1).astype(F32)
        for b in range(16):
            span = pl.ds(b * 128, 128)
            cols_hot[span, :] = jnp.where(
                jnp.broadcast_to(columns[:, b : b + 1], (128, COLS)) == wide, 1.0, 0.0
            ).astype(BF16)
            rows_t[:, span] = lax.dot_general(
                eye, rows_ref[span, :], (((1,), (1,)), ((), ())), preferred_element_type=F32
            ).astype(BF16)
        thick = jnp.transpose(jnp.broadcast_to(thick_ref[...], (128, 128)))
        thick_full[:, 0:128] = thick
        thick_full[:, 128:256] = thick
        pl.semaphore_wait(barrier, 6)

        @pl.when(has_north)
        def _():
            next_copy(0).start()

    base = (step * 8).astype(F32)
    row_ids = row_of[...]
    for r in range(8):
        mask = jnp.where(row_ids == base + float(r), 1.0, 0.0).astype(BF16)
        masked[pl.ds(r * 128, 128), :] = rows_t[...] * mask
    forced[...] = jnp.dot(masked[...], cols_hot[...], preferred_element_type=F32)
    levels = iota((LEV, COLS), 0)
    flat_field = field_ref.reshape(2048, 128)

    def row(r, carry):
        adjoint = jnp.concatenate(
            [flat_field[pl.ds(r, 128, stride=16), :], flat_field[pl.ds(8 + r, 128, stride=16), :]], axis=1
        )
        start = pl.multiple_of(r * 128, 128)
        value = adjoint + forced[pl.ds(start, 128), :]
        matrix = mixing_ref[r]
        v_hi = value.astype(BF16)
        v_lo = (value - v_hi.astype(F32)).astype(BF16)
        m_hi = matrix.astype(BF16)
        m_lo = (matrix - m_hi.astype(F32)).astype(BF16)
        mixed = (
            jnp.dot(m_hi, v_lo, preferred_element_type=F32)
            + jnp.dot(m_lo, v_hi, preferred_element_type=F32)
        ) + jnp.dot(m_hi, v_hi, preferred_element_type=F32)
        cloudy = levels < top_ref[pl.ds(r, 1), :]
        thick = thick_full[...]
        total = jnp.sum(jnp.where(cloudy, mixed, 0.0), axis=0, keepdims=True)
        mass = jnp.sum(jnp.where(cloudy, thick, 0.0), axis=0, keepdims=True)
        fraction = frac_ref[pl.ds(r, 1), :]
        convected = jnp.where(cloudy, mixed + fraction * (thick * (total / mass) - mixed), mixed)
        out_ref[r] = convected
        low = convected[0:64, 0:128]
        high = pltpu.roll(convected[64:128, 0:128], PACK, 1)
        edge[step * 8 + r] = jnp.where(iota((64, 128), 1) < PACK, low, high)
        return carry

    lax.fori_loop(0, 8, row, 0)
    halo_copy(step).start()

    @pl.when((step == 0) & has_north)
    def _():
        first[...] = out_ref[0]
        next_copy(1).start()
        next_copy(2).start()

    @pl.when(step == 3)
    def _():
        @pl.when(has_north)
        def _():
            for which in range(3):
                next_copy(which).wait_send()

        @pl.when(has_south)
        def _():
            for which in range(3):
                next_copy(which).wait_recv()

        for block in range(4):
            halo_copy(block).wait()


def column_step(rows, meta, field, mixing, top, frac, thick, courant, shift, zfrac):
    whole = lambda *shape: pl.BlockSpec(shape, lambda i: (0,) * len(shape))
    anywhere = pl.BlockSpec(memory_space=pl.ANY)
    return pl.pallas_call(
        column_kernel,
        grid=(4,),
        out_shape=[
            jax.ShapeDtypeStruct((ROWS, LEV, COLS), F32),
            jax.ShapeDtypeStruct((ROWS, 64, 128), F32),
            jax.ShapeDtypeStruct((LEV, COLS), F32),
            jax.ShapeDtypeStruct((64, 128), F32),
            jax.ShapeDtypeStruct((LEV, 512), F32),
        ],
        in_specs=[
            whole(OBS, LEV),
            whole(NDEV, 128),
            pl.BlockSpec((LEV, 1, 16, 128), lambda i: (0, i, 0, 0)),
            pl.BlockSpec((8, LEV, LEV), lambda i: (i, 0, 0)),
            pl.BlockSpec((8, COLS), lambda i: (i, 0)),
            pl.BlockSpec((8, COLS), lambda i: (i, 0)),
            whole(1, LEV),
            pl.BlockSpec((LEV, 1, 16, 128), lambda i: (0, 0, 0, 0)),
            whole(ROWS, LEV),
            whole(ROWS, LEV),
        ],
        out_specs=[pl.BlockSpec((8, LEV, COLS), lambda i: (i, 0, 0))] + [anywhere] * 4,
        scratch_shapes=[
            pltpu.VMEM((LEV, OBS), BF16),
            pltpu.VMEM((OBS, COLS), BF16),
            pltpu.VMEM((1, OBS), F32),
            pltpu.VMEM((LEV, COLS), F32),
            pltpu.VMEM((8 * LEV, OBS), BF16),
            pltpu.VMEM((8 * LEV, COLS), F32),
            pltpu.VMEM((LEV, 512), F32),
            pltpu.VMEM((LEV, COLS), F32),
            pltpu.VMEM((ROWS, 64, 128), F32),
            DMA((2, 4)),
            DMA((2, 3)),
        ],
        compiler_params=pltpu.CompilerParams(
            vmem_limit_bytes=56 * 1024 * 1024, collective_id=1, has_side_effects=True
        ),
        name="column",
    )(rows, meta, field, mixing, top, frac, thick, courant, shift, zfrac)


def transport_kernel(
    conv_ref, halo_ref, next_conv_ref, next_halo_ref, next_given_ref,
    shift_ref, frac_ref, courant_ref, out_ref, shift_pad, frac_pad, carried,
):
    step = pl.program_id(0)
    lane = iota((LEV, 128), 1)
    tail = jnp.where(iota((LEV, 128), 0) < 64, 0, PACK)

    def zonal(first, second, packed, shift, fraction):
        def pick(offset):
            index = lane + offset
            inside = index < 128
            wrapped = index & 127
            a = jnp.take_along_axis(first, wrapped, axis=1)
            b = jnp.take_along_axis(second, wrapped, axis=1)
            c = jnp.take_along_axis(packed, (wrapped + tail) & 127, axis=1)
            return jnp.where(inside, a, b), jnp.where(inside, b, c)

        left, right = pick(shift)
        left_next, right_next = pick(shift + 1)
        keep = 1.0 - fraction
        return keep * left + fraction * left_next, keep * right + fraction * right_next

    def doubled(packed):
        return jnp.concatenate([packed, packed], axis=0)

    @pl.when(step == 0)
    def _():
        rest = jnp.zeros((LEV - ROWS, 128), F32)
        shifts = jnp.concatenate([shift_ref[...].astype(F32), rest], axis=0)
        shift_pad[...] = jnp.transpose(shifts).astype(I32)
        frac_pad[...] = jnp.transpose(jnp.concatenate([frac_ref[...], rest], axis=0))
        last = lax.axis_index("lat") == NLAT - 1
        shift = jnp.clip(next_given_ref[:, 256:384], 0.0, float(SHIFT_MAX)).astype(I32)
        fraction = next_given_ref[:, 384:512]
        left, right = zonal(
            next_conv_ref[:, 0:128], next_conv_ref[:, 128:256], doubled(next_halo_ref[...]), shift, fraction
        )
        carried[:, 0:128] = jnp.where(last, 0.0, next_given_ref[:, 0:128] * left)
        carried[:, 128:256] = jnp.where(last, 0.0, next_given_ref[:, 128:256] * right)

    flat_courant = courant_ref.reshape(2048, 128)
    flat_out = out_ref.reshape(2048, 128)
    first_row = (3 - step) * 8

    def row(back, carry):
        r = 7 - back
        here = jnp.full((LEV, 128), first_row + r, I32)
        shift = jnp.take_along_axis(shift_pad[...], here, axis=1)
        fraction = jnp.take_along_axis(frac_pad[...], here, axis=1)
        parts = zonal(
            conv_ref[r, :, 0:128], conv_ref[r, :, 128:256], doubled(halo_ref[r]), shift, fraction
        )
        for half in range(2):
            at = pl.ds(half * 8 + r, 128, stride=16)
            span = pl.ds(half * 128, 128)
            moved = flat_courant[at, :] * parts[half]
            flat_out[at, :] = parts[half] - moved + carried[:, span]
            carried[:, span] = moved
        return carry

    lax.fori_loop(0, 8, row, 0)


def transport(conv, halo, next_conv, next_halo, next_given, shift, frac, courant):
    whole = lambda *shape: pl.BlockSpec(shape, lambda i: (0,) * len(shape))
    blocked = pl.BlockSpec((LEV, 1, 16, 128), lambda i: (0, 3 - i, 0, 0))
    return pl.pallas_call(
        transport_kernel,
        grid=(4,),
        out_shape=jax.ShapeDtypeStruct((LEV, 4, 16, 128), F32),
        in_specs=[
            pl.BlockSpec((8, LEV, COLS), lambda i: (3 - i, 0, 0)),
            pl.BlockSpec((8, 64, 128), lambda i: (3 - i, 0, 0)),
            whole(LEV, COLS),
            whole(64, 128),
            whole(LEV, 512),
            whole(ROWS, LEV),
            whole(ROWS, LEV),
            blocked,
        ],
        out_specs=blocked,
        scratch_shapes=[
            pltpu.VMEM((LEV, 128), I32),
            pltpu.VMEM((LEV, 128), F32),
            pltpu.VMEM((LEV, COLS), F32),
        ],
        compiler_params=pltpu.CompilerParams(vmem_limit_bytes=60 * 1024 * 1024),
        name="transport",
    )(conv, halo, next_conv, next_halo, next_given, shift, frac, courant)


def tiles(value):
    return value.reshape(LEV, 4, 8, 2, 128).transpose(0, 1, 3, 2, 4).reshape(LEV, 4, 16, 128)


def untiles(value):
    return value.reshape(LEV, 4, 2, 8, 128).transpose(0, 1, 3, 2, 4).reshape(LEV, ROWS, COLS)


def shards(
    adjoint_field, mixing_inverse, cloud_top, conv_frac, thickness, zonal_shift, zonal_frac,
    merid_courant, obs_kernel, obs_depart, obs_dest, obs_col, obs_count,
):
    courant = tiles(merid_courant)
    shift, zfrac = zonal_shift.T, zonal_frac.T
    rows, meta = exchange(obs_count, obs_kernel, obs_depart, obs_dest, obs_col)
    conv, halo, next_conv, next_halo, next_given = column_step(
        rows.reshape(OBS, LEV), meta.reshape(NDEV, 128), tiles(adjoint_field), mixing_inverse,
        cloud_top, conv_frac, thickness.reshape(1, LEV), courant, shift, zfrac,
    )
    out = transport(conv, halo, next_conv, next_halo, next_given, shift, zfrac, courant)
    return untiles(out)


def solution(mesh):
    split = P(None, "lat", "lon")
    both = P(("lat", "lon"))
    return jax.shard_map(
        shards,
        mesh=mesh,
        in_specs=(
            split, P("lat", None, None), P("lat", "lon"), P("lat", "lon"), P(), P(None, "lat"), P(None, "lat"),
            split, P(("lat", "lon"), None), both, both, both, both,
        ),
        out_specs=split,
        check_vma=False,
    )
```

```python
import functools

import jax
import jax.numpy as jnp
from jax import lax
from jax.experimental import pallas as pl
from jax.experimental.pallas import tpu as pltpu
from jax.sharding import PartitionSpec as P

MESH = pl.DeviceIdType.MESH
F32 = jnp.float32
BF16 = jnp.bfloat16
I32 = jnp.int32
DMA = pltpu.SemaphoreType.DMA
NLAT, NLON, NDEV = 8, 16, 128
LEV, ROWS, COLS = 128, 32, 256
OBS, CAP = 2048, 16
PACK = 64
PART = 32
GROUP = 2
AHEAD = 4
UNROLL = 4


def iota(shape, axis):
    return lax.broadcasted_iota(I32, shape, axis)


def exchange_kernel(
    count_ref, kernel_ref, depart_ref, dest_ref, col_ref, rows_out, meta_out,
    send_rows, send_meta, contribution, entered, sems,
):
    lat, lon = lax.axis_index("lat"), lax.axis_index("lon")
    me = lat * NLON + lon
    barrier = pltpu.get_barrier_semaphore()

    def greet(target_of, semaphore, count):
        def body(step, carry):
            pl.semaphore_signal(semaphore, inc=1, device_id=target_of(step), device_id_type=MESH)
            return carry

        lax.fori_loop(1, count, body, 0)

    lon_peer = lambda step: (lat, lax.rem(lon + step, NLON))
    lat_peer = lambda step: (lax.rem(lat + step, NLAT), lon)
    greet(lon_peer, barrier, NLON)
    greet(lat_peer, barrier, NLAT)

    dest = dest_ref[...]
    sub, lane = iota((16, 128), 0), iota((16, 128), 1)
    flat = sub * 128 + lane
    rank = jnp.zeros((16, 128), I32)
    for step in range(1, CAP):
        rolled = pltpu.roll(dest, step, 1)
        before = jnp.where(lane < step, pltpu.roll(rolled, 1, 0), rolled)
        rank = rank + jnp.where((before == dest) & (flat >= step), 1, 0)
    live = flat < count_ref[0]
    slot = jnp.where(live, dest * CAP + rank, -1)
    dest_live = jnp.where(live, dest, -1)
    cells = col_ref[...]
    cell_row = (cells // COLS).astype(F32)
    cell_col = (cells % COLS).astype(F32)

    depart_t = jnp.transpose(depart_ref[...])
    for block in range(16):
        span = pl.ds(block * 128, 128)
        contribution[span, :] = (
            kernel_ref[span, :].astype(F32) * jnp.broadcast_to(depart_t[:, block : block + 1], (128, 128))
        ).astype(BF16)

    pl.semaphore_wait(barrier, NLON + NLAT - 2)
    greet(lat_peer, entered, NLAT)

    big_sub = iota((128, 128), 0)
    mine = (big_sub // CAP) == lax.rem(me, 8)
    meta = jnp.zeros((128, 128), F32)
    nt = (((1,), (1,)), ((), ()))
    for block in range(16):
        owner = jnp.where(dest_live[block : block + 1, :] == big_sub, 1.0, 0.0).astype(BF16)
        place = (rank[block : block + 1, :] == big_sub % CAP) & mine
        row_part = jnp.where(place, cell_row[block : block + 1, :], 0.0).astype(BF16)
        col_part = jnp.where(place, cell_col[block : block + 1, :], 0.0).astype(BF16)
        meta = meta + float(COLS) * lax.dot_general(owner, row_part, nt, preferred_element_type=F32)
        meta = meta + lax.dot_general(owner, col_part, nt, preferred_element_type=F32)
    meta = meta.astype(I32)
    for dst in range(NDEV):
        send_meta[dst, :, :] = meta[dst : dst + 1, :]

    for out_block in range(16):
        total = jnp.zeros((128, 128), F32)
        for block in range(out_block + 1):
            hit = jnp.where(slot[block : block + 1, :] == big_sub + out_block * 128, 1.0, 0.0).astype(BF16)
            total = total + jnp.dot(
                hit, contribution[pl.ds(block * 128, 128), :], preferred_element_type=F32
            )
        send_rows[pl.ds(out_block * 8, 8), :, :] = total.astype(BF16).reshape(8, CAP, LEV)

    pl.semaphore_wait(entered, NLAT - 1)

    def send(step, carry):
        target = lax.rem(me + step, NDEV)
        where = (target // NLON, lax.rem(target, NLON))
        pltpu.make_async_remote_copy(
            send_rows.at[target], rows_out.at[me], sems.at[0], sems.at[1],
            device_id=where, device_id_type=MESH,
        ).start()
        pltpu.make_async_remote_copy(
            send_meta.at[target], meta_out.at[me], sems.at[2], sems.at[3],
            device_id=where, device_id_type=MESH,
        ).start()
        return carry

    lax.fori_loop(1, NDEV, send, 0)
    own_rows = pltpu.make_async_copy(send_rows.at[me], rows_out.at[me], sems.at[4])
    own_meta = pltpu.make_async_copy(send_meta.at[me], meta_out.at[me], sems.at[5])
    own_rows.start()
    own_meta.start()
    own_rows.wait()
    own_meta.wait()
    others = pl.ds(0, NDEV - 1)
    pltpu.make_async_copy(send_rows.at[others], send_rows.at[others], sems.at[0]).wait()
    pltpu.make_async_copy(send_meta.at[others], send_meta.at[others], sems.at[2]).wait()
    pltpu.make_async_copy(rows_out.at[others], rows_out.at[others], sems.at[1]).wait()
    pltpu.make_async_copy(meta_out.at[others], meta_out.at[others], sems.at[3]).wait()


def exchange(obs_count, obs_kernel, obs_depart, obs_dest, obs_col):
    vmem = pl.BlockSpec(memory_space=pltpu.VMEM)
    return pl.pallas_call(
        exchange_kernel,
        out_shape=[
            jax.ShapeDtypeStruct((NDEV, CAP, LEV), BF16),
            jax.ShapeDtypeStruct((NDEV, 1, 128), I32),
        ],
        in_specs=[pl.BlockSpec(memory_space=pltpu.SMEM)] + [vmem] * 4,
        out_specs=[vmem, vmem],
        scratch_shapes=[
            pltpu.VMEM((NDEV, CAP, LEV), BF16),
            pltpu.VMEM((NDEV, 1, 128), I32),
            pltpu.VMEM((OBS, LEV), BF16),
            pltpu.SemaphoreType.REGULAR,
            DMA((6,)),
        ],
        compiler_params=pltpu.CompilerParams(collective_id=0, has_side_effects=True),
        name="exchange",
    )(
        obs_count, obs_kernel, obs_depart.reshape(16, 128),
        obs_dest.reshape(16, 128), obs_col.reshape(16, 128),
    )


def column_kernel(
    rows_ref, meta_ref, field_hbm, mixing_ref, top_ref, frac_ref, thick_ref, courant_ref, shift_ref, zfrac_ref,
    out_ref, halo_in, next_in, next_halo_in, next_given_in,
    rows_t, cols_hot, row_of, thick_full, forced, given, first, edge, field, mass, weights, halo_sems, next_sems,
    field_sems,
):
    step = pl.program_id(0)
    lat, lon = lax.axis_index("lat"), lax.axis_index("lon")
    west = lax.rem(lon + NLON - 1, NLON)
    east = lax.rem(lon + 1, NLON)
    north = lax.rem(lat + NLAT - 1, NLAT)
    has_north, has_south = lat > 0, lat < NLAT - 1

    def halo_copy(block):
        return pltpu.make_async_remote_copy(
            edge.at[pl.ds(block * 8, 8)], halo_in.at[pl.ds(block * 8, 8)],
            halo_sems.at[0, block], halo_sems.at[1, block], device_id=(lat, west), device_id_type=MESH,
        )

    def next_copy(which):
        source = (given, first, edge.at[0])[which]
        target = (next_given_in, next_in, next_halo_in)[which]
        column = (lon, lon, west)[which]
        return pltpu.make_async_remote_copy(
            source, target, next_sems.at[0, which], next_sems.at[1, which],
            device_id=(north, column), device_id_type=MESH,
        )

    @pl.when(step == 0)
    def _():
        def fetch(row, carry):
            for half in range(2):
                pltpu.make_async_copy(
                    field_hbm.at[:, place(row, half), :], field.at[row, half], field_sems.at[row // 8]
                ).start()
            return carry

        lax.fori_loop(0, ROWS, fetch, 0)
        barrier = pltpu.get_barrier_semaphore()
        south = lax.rem(lat + 1, NLAT)
        for target in (
            (lat, west), (lat, east), (north, lon), (south, lon), (north, west), (south, east)
        ):
            pl.semaphore_signal(barrier, inc=1, device_id=target, device_id_type=MESH)
        flat_courant = courant_ref.reshape(2048, 128)
        given[0:128, 0:128] = flat_courant[pl.ds(0, 128, stride=16), :]
        given[0:128, 128:256] = flat_courant[pl.ds(8, 128, stride=16), :]
        given[128:136, 0:128] = shift_ref[0:8, :].astype(F32)
        given[128:136, 128:256] = jnp.zeros((8, 128), F32)
        blank = jnp.zeros((LEV - ROWS, 128), F32)
        weights[...] = jnp.transpose(jnp.concatenate([zfrac_ref[...], blank], axis=0))
        cells = jnp.sum(meta_ref[...].reshape(16, 8, 128), axis=1)
        cell_rows = (cells // COLS).astype(F32)
        columns = jnp.transpose((cells % COLS).astype(F32))
        eye = jnp.where(iota((128, 128), 0) == iota((128, 128), 1), 1.0, 0.0).astype(BF16)
        wide = iota((128, COLS), 1).astype(F32)
        for b in range(16):
            row_of[:, b * 128 : b * 128 + 128] = cell_rows[b : b + 1, :]
            span = pl.ds(b * 128, 128)
            cols_hot[span, :] = jnp.where(
                jnp.broadcast_to(columns[:, b : b + 1], (128, COLS)) == wide, 1.0, 0.0
            ).astype(BF16)
            rows_t[:, span] = lax.dot_general(
                eye, rows_ref[span, :], (((1,), (1,)), ((), ())), preferred_element_type=F32
            )
        thick = jnp.transpose(jnp.broadcast_to(thick_ref[...], (128, 128)))
        thick_full[...] = thick
        below = jnp.where(iota((128, 128), 0) <= iota((128, 128), 1), thick, 0.0)
        sums = jnp.broadcast_to(jnp.sum(below, axis=0, keepdims=True), (ROWS, 128))
        for half in range(2):
            span = pl.ds(half * 128, 128)
            mass[:, span] = jnp.take_along_axis(sums, top_ref[:, span] - 1, axis=1, mode="promise_in_bounds")
        pl.semaphore_wait(barrier, 6)

        @pl.when(has_north)
        def _():
            next_copy(0).start()

    base = (step * 8).astype(F32)
    row_ids = row_of[...]
    pieces = [jnp.where(row_ids == base + float(r), rows_t[...], 0.0).astype(BF16) for r in range(8)]
    forced[...] = jnp.dot(jnp.concatenate(pieces, axis=0), cols_hot[...], preferred_element_type=F32)
    lane = iota((LEV, 128), 1)
    low_lane = (lane[0:64, :] < PACK - 1) | (lane[0:64, :] == 127)
    here = pl.ds(step * 8, 8)
    pltpu.make_async_copy(field.at[here], field.at[here], field_sems.at[step]).wait()
    levels = iota((LEV, 128), 0)

    def one_row(r):
        row = step * 8 + r
        tops, fractions, masses = (ref[pl.ds(row, 1), :] for ref in (top_ref, frac_ref, mass))
        matrix = mixing_ref[r]
        m_hi = matrix.astype(BF16)
        m_lo = (matrix - m_hi.astype(F32)).astype(BF16)
        left = jnp.concatenate([m_hi, m_lo, m_hi], axis=1)
        parts = []
        for half in range(2):
            span = pl.ds(half * 128, 128)
            start = pl.multiple_of(r * 128, 128)
            value = field[row, half] + forced[pl.ds(start, 128), span]
            v_hi = value.astype(BF16)
            v_lo = (value - v_hi.astype(F32)).astype(BF16)
            mixed = jnp.dot(left, jnp.concatenate([v_hi, v_hi, v_lo], axis=0), preferred_element_type=F32)
            cloudy = levels < tops[:, half * 128 : half * 128 + 128]
            total = jnp.sum(jnp.where(cloudy, mixed, 0.0), axis=0, keepdims=True)
            fraction = fractions[:, half * 128 : half * 128 + 128]
            share = fraction * (total / masses[:, half * 128 : half * 128 + 128])
            convected = jnp.where(cloudy, mixed * (1.0 - fraction) + thick_full[...] * share, mixed)
            parts.append(convected)
        weight = jnp.take_along_axis(
            weights[...], jnp.full((LEV, 128), row, I32), axis=1, mode="promise_in_bounds"
        )
        turned = [pltpu.roll(part, 127, 1) for part in parts]
        between = parts[0] + weight * (jnp.where(lane == 127, turned[1], turned[0]) - parts[0])
        out_ref[r, :, 0:128] = between
        out_ref[r, :, 128:256] = parts[1] + weight * (jnp.where(lane == 127, 0.0, turned[1]) - parts[1])
        sent = jnp.where(lane == 127, weight * turned[0], between)
        edge[row] = jnp.where(low_lane, sent[0:64, :], pltpu.roll(sent[64:128, :], PACK, 1)).astype(BF16)

    def rows_of(pair, carry):
        for i in range(UNROLL):
            one_row(pair * UNROLL + i)
        return carry

    lax.fori_loop(0, 8 // UNROLL, rows_of, 0)
    halo_copy(step).start()

    @pl.when((step == 0) & has_north)
    def _():
        first[...] = out_ref[0]
        next_copy(1).start()
        next_copy(2).start()

    @pl.when(step == 3)
    def _():
        @pl.when(has_north)
        def _():
            for which in range(3):
                next_copy(which).wait_send()

        @pl.when(has_south)
        def _():
            for which in range(3):
                next_copy(which).wait_recv()

        for block in range(4):
            halo_copy(block).wait()


def column_step(rows, meta, field, mixing, top, frac, thick, courant, shift, zfrac):
    whole = lambda *shape: pl.BlockSpec(shape, lambda i: (0,) * len(shape))
    anywhere = pl.BlockSpec(memory_space=pl.ANY)
    return pl.pallas_call(
        column_kernel,
        grid=(4,),
        out_shape=[
            jax.ShapeDtypeStruct((ROWS, LEV, COLS), F32),
            jax.ShapeDtypeStruct((ROWS, 64, 128), BF16),
            jax.ShapeDtypeStruct((LEV, COLS), F32),
            jax.ShapeDtypeStruct((64, 128), BF16),
            jax.ShapeDtypeStruct((LEV + 8, COLS), F32),
        ],
        in_specs=[
            whole(OBS, LEV),
            whole(NDEV, 128),
            anywhere,
            pl.BlockSpec((8, LEV, LEV), lambda i: (i, 0, 0)),
            whole(ROWS, COLS),
            whole(ROWS, COLS),
            whole(1, LEV),
            pl.BlockSpec((LEV, 1, 16, 128), lambda i: (0, 0, 0, 0)),
            whole(ROWS, LEV),
            whole(ROWS, LEV),
        ],
        out_specs=[pl.BlockSpec((8, LEV, COLS), lambda i: (i, 0, 0))] + [anywhere] * 4,
        scratch_shapes=[
            pltpu.VMEM((LEV, OBS), F32),
            pltpu.VMEM((OBS, COLS), BF16),
            pltpu.VMEM((1, OBS), F32),
            pltpu.VMEM((LEV, 128), F32),
            pltpu.VMEM((8 * LEV, COLS), F32),
            pltpu.VMEM((LEV + 8, COLS), F32),
            pltpu.VMEM((LEV, COLS), F32),
            pltpu.VMEM((ROWS, 64, 128), BF16),
            pltpu.VMEM((ROWS, 2, LEV, 128), F32),
            pltpu.VMEM((ROWS, COLS), F32),
            pltpu.VMEM((LEV, 128), F32),
            DMA((2, 4)),
            DMA((2, 3)),
            DMA((4,)),
        ],
        compiler_params=pltpu.CompilerParams(
            vmem_limit_bytes=56 * 1024 * 1024, collective_id=1, has_side_effects=True
        ),
        name="column",
    )(rows, meta, field.reshape(LEV, 64, 128), mixing, top, frac, thick, courant, shift, zfrac)


def place(row, half):
    return row // 8 * 16 + half * 8 + row % 8


def transport_kernel(
    conv_hbm, halo_hbm, next_conv_ref, next_halo_ref, next_given_ref, shift_ref, courant_hbm, out_hbm,
    conv, halo, courant, out, shifts, moved, conv_sems, courant_sems, halo_sems, out_sem,
):
    last = lax.axis_index("lat") == NLAT - 1
    groups = ROWS // GROUP

    def conv_copy(group):
        rows = pl.ds(group * GROUP, GROUP)
        return pltpu.make_async_copy(conv_hbm.at[rows], conv.at[rows], conv_sems.at[group])

    def halo_copy(group):
        rows = pl.ds(group * GROUP, GROUP)
        return pltpu.make_async_copy(halo_hbm.at[rows], halo.at[rows], halo_sems.at[group])

    def fetch(group):
        conv_copy(group).start()
        halo_copy(group).start()
        for i in range(GROUP):
            row = group * GROUP + i
            for half in range(2):
                pltpu.make_async_copy(
                    courant_hbm.at[:, place(row, half), :], courant.at[row, half], courant_sems.at[group]
                ).start()

    for ahead in range(AHEAD):
        fetch(groups - 1 - ahead)

    given = jnp.where(last, 0.0, next_given_ref[128:136, :])
    blank = jnp.zeros((LEV - ROWS - 1, 128), F32)
    shifts[...] = jnp.transpose(
        jnp.concatenate([shift_ref[...].astype(F32), given[0:1, 0:128], blank], axis=0)
    ).astype(I32)
    lane = iota((PART, 128), 1)

    def lanes(values, index):
        return jnp.take_along_axis(values, index, axis=1, mode="promise_in_bounds")

    def zonal(first, second, packed, part, row):
        levels = pl.ds(part * PART, PART)
        third = packed[pl.ds(part * PART % 64, PART), :].astype(F32)
        if part * PART >= 64:
            third = pltpu.roll(third, PACK, 1)
        here = jnp.full((PART, 128), row, I32)
        shift = lanes(shifts[levels, :], here)
        second = second + jnp.where(lane == 127, third, 0.0)
        index = lane + shift
        wrapped = index & 127
        a = lanes(jnp.where(lane < shift, third, first), wrapped)
        b = lanes(second, wrapped)
        inside = index < 128
        return jnp.where(inside, a, b), jnp.where(inside, b, a)

    for part in range(LEV // PART):
        levels = pl.ds(part * PART, PART)
        both = zonal(next_conv_ref[levels, 0:128], next_conv_ref[levels, 128:256], next_halo_ref, part, ROWS)
        for half in range(2):
            span = pl.ds(half * 128, 128)
            moved[half, levels, :] = jnp.where(last, 0.0, next_given_ref[levels, span] * both[half])
    def step(back, carry):
        group = groups - 1 - back
        rows = pl.ds(group * GROUP, GROUP)

        @pl.when(group >= AHEAD)
        def _():
            fetch(group - AHEAD)

        conv_copy(group).wait()
        halo_copy(group).wait()
        pltpu.make_async_copy(courant.at[rows], courant.at[rows], courant_sems.at[group]).wait()
        for part in range(LEV // PART):
            levels = pl.ds(part * PART, PART)
            coming = [moved[0, levels, :], moved[1, levels, :]]
            for i in reversed(range(GROUP)):
                row = group * GROUP + i
                both = zonal(conv[row, levels, 0:128], conv[row, levels, 128:256], halo.at[row], part, row)
                for half in range(2):
                    leaving = courant[row, half, levels, :] * both[half]
                    out[row, half, levels, :] = both[half] - leaving + coming[half]
                    coming[half] = leaving
            for half in range(2):
                moved[half, levels, :] = coming[half]
        for i in range(GROUP):
            row = group * GROUP + i
            for half in range(2):
                pltpu.make_async_copy(
                    out.at[row, half], out_hbm.at[:, place(row, half), :], out_sem
                ).start()
        return carry

    lax.fori_loop(0, groups, step, 0)
    pltpu.make_async_copy(out, out, out_sem).wait()


def transport(conv, halo, next_conv, next_halo, next_given, shift, courant):
    vmem = pl.BlockSpec(memory_space=pltpu.VMEM)
    anywhere = pl.BlockSpec(memory_space=pl.ANY)
    return pl.pallas_call(
        transport_kernel,
        out_shape=jax.ShapeDtypeStruct((LEV, 64, 128), F32),
        in_specs=[anywhere, anywhere] + [vmem] * 4 + [anywhere],
        out_specs=anywhere,
        scratch_shapes=[
            pltpu.VMEM((ROWS, LEV, COLS), F32),
            pltpu.VMEM((ROWS, 64, 128), BF16),
            pltpu.VMEM((ROWS, 2, LEV, 128), F32),
            pltpu.VMEM((ROWS, 2, LEV, 128), F32),
            pltpu.VMEM((LEV, 128), I32),
            pltpu.VMEM((2, LEV, 128), F32),
            DMA((ROWS // GROUP,)),
            DMA((ROWS // GROUP,)),
            DMA((ROWS // GROUP,)),
            DMA,
        ],
        compiler_params=pltpu.CompilerParams(vmem_limit_bytes=60 * 1024 * 1024),
        name="transport",
    )(conv, halo, next_conv, next_halo, next_given, shift, courant.reshape(LEV, 64, 128))


def tiles(value):
    return value.reshape(LEV, 4, 8, 2, 128).transpose(0, 1, 3, 2, 4).reshape(LEV, 4, 16, 128)


def untiles(value):
    return value.reshape(LEV, 4, 2, 8, 128).transpose(0, 1, 3, 2, 4).reshape(LEV, ROWS, COLS)


def shards(
    adjoint_field, mixing_inverse, cloud_top, conv_frac, thickness, zonal_shift, zonal_frac,
    merid_courant, obs_kernel, obs_depart, obs_dest, obs_col, obs_count,
):
    courant = tiles(merid_courant)
    shift, zfrac = zonal_shift.T, zonal_frac.T
    rows, meta = exchange(obs_count, obs_kernel, obs_depart, obs_dest, obs_col)
    conv, halo, next_conv, next_halo, next_given = column_step(
        rows.reshape(OBS, LEV), meta.reshape(NDEV, 128), tiles(adjoint_field), mixing_inverse,
        cloud_top, conv_frac, thickness.reshape(1, LEV), courant, shift, zfrac,
    )
    out = transport(conv, halo, next_conv, next_halo, next_given, shift, courant)
    return untiles(out)


def solution(mesh):
    split = P(None, "lat", "lon")
    both = P(("lat", "lon"))
    return jax.shard_map(
        shards,
        mesh=mesh,
        in_specs=(
            split, P("lat", None, None), P("lat", "lon"), P("lat", "lon"), P(), P(None, "lat"), P(None, "lat"),
            split, P(("lat", "lon"), None), both, both, both, both,
        ),
        out_specs=split,
        check_vma=False,
    )
```

```python
import functools

import jax
import jax.numpy as jnp
from jax import lax
from jax.experimental import pallas as pl
from jax.experimental.pallas import tpu as pltpu
from jax.sharding import PartitionSpec as P

MESH = pl.DeviceIdType.MESH
F32 = jnp.float32
BF16 = jnp.bfloat16
I32 = jnp.int32
DMA = pltpu.SemaphoreType.DMA
NLAT, NLON, NDEV = 8, 16, 128
LEV, ROWS, COLS = 128, 32, 256
OBS, CAP = 2048, 16
PACK = 64
PART = 16
GROUP = 2
AHEAD = 4
UNROLL = 4


def iota(shape, axis):
    return lax.broadcasted_iota(I32, shape, axis)


def exchange_kernel(
    count_ref, kernel_ref, depart_ref, dest_ref, col_ref, rows_out, meta_out,
    send_rows, send_meta, contribution, entered, sems,
):
    lat, lon = lax.axis_index("lat"), lax.axis_index("lon")
    me = lat * NLON + lon
    barrier = pltpu.get_barrier_semaphore()

    def greet(target_of, semaphore, count):
        def body(step, carry):
            pl.semaphore_signal(semaphore, inc=1, device_id=target_of(step), device_id_type=MESH)
            return carry

        lax.fori_loop(1, count, body, 0)

    lon_peer = lambda step: (lat, lax.rem(lon + step, NLON))
    lat_peer = lambda step: (lax.rem(lat + step, NLAT), lon)
    greet(lon_peer, barrier, NLON)
    greet(lat_peer, barrier, NLAT)

    dest = dest_ref[...]
    sub, lane = iota((16, 128), 0), iota((16, 128), 1)
    flat = sub * 128 + lane
    rank = jnp.zeros((16, 128), I32)
    for step in range(1, CAP):
        rolled = pltpu.roll(dest, step, 1)
        before = jnp.where(lane < step, pltpu.roll(rolled, 1, 0), rolled)
        rank = rank + jnp.where((before == dest) & (flat >= step), 1, 0)
    live = flat < count_ref[0]
    slot = jnp.where(live, dest * CAP + rank, -1)
    dest_live = jnp.where(live, dest, -1)
    cells = col_ref[...]
    cell_row = (cells // COLS).astype(F32)
    cell_col = (cells % COLS).astype(F32)

    depart_t = jnp.transpose(depart_ref[...])
    for block in range(16):
        span = pl.ds(block * 128, 128)
        contribution[span, :] = (
            kernel_ref[span, :].astype(F32) * jnp.broadcast_to(depart_t[:, block : block + 1], (128, 128))
        ).astype(BF16)

    pl.semaphore_wait(barrier, NLON + NLAT - 2)
    greet(lat_peer, entered.at[lat], NLAT)

    big_sub = iota((128, 128), 0)
    mine = (big_sub // CAP) == lax.rem(me, 8)
    meta = jnp.zeros((128, 128), F32)
    nt = (((1,), (1,)), ((), ()))
    for block in range(16):
        owner = jnp.where(dest_live[block : block + 1, :] == big_sub, 1.0, 0.0).astype(BF16)
        place = (rank[block : block + 1, :] == big_sub % CAP) & mine
        row_part = jnp.where(place, cell_row[block : block + 1, :], 0.0).astype(BF16)
        col_part = jnp.where(place, cell_col[block : block + 1, :], 0.0).astype(BF16)
        meta = meta + float(COLS) * lax.dot_general(owner, row_part, nt, preferred_element_type=F32)
        meta = meta + lax.dot_general(owner, col_part, nt, preferred_element_type=F32)
    meta = meta.astype(I32)
    for dst in range(NDEV):
        send_meta[dst, :, :] = meta[dst : dst + 1, :]

    slots = jnp.concatenate([slot[block : block + 1, :] for block in range(16)], axis=1)
    for out_block in range(16):
        width = (out_block + 1) * 128
        hit = jnp.where(slots[:, 0:width] - out_block * 128 == iota((128, width), 0), 1.0, 0.0).astype(BF16)
        total = jnp.dot(hit, contribution[0:width, :], preferred_element_type=F32)
        send_rows[pl.ds(out_block * 8, 8), :, :] = total.astype(BF16).reshape(8, CAP, LEV)

    def send_to(to_lat, to_lon):
        target = to_lat * NLON + to_lon
        pltpu.make_async_remote_copy(
            send_rows.at[target], rows_out.at[me], sems.at[0], sems.at[1],
            device_id=(to_lat, to_lon), device_id_type=MESH,
        ).start()
        pltpu.make_async_remote_copy(
            send_meta.at[target], meta_out.at[me], sems.at[2], sems.at[3],
            device_id=(to_lat, to_lon), device_id_type=MESH,
        ).start()

    def send_near(step, carry):
        send_to(lat, lax.rem(lon + step, NLON))
        return carry

    lax.fori_loop(1, NLON, send_near, 0)

    def send_row(step, carry):
        to_lat = lax.rem(lat + step, NLAT)
        pl.semaphore_wait(entered.at[to_lat], 1)

        def send_far(turn, inner):
            send_to(to_lat, lax.rem(lon + turn, NLON))
            return inner

        return lax.fori_loop(0, NLON, send_far, carry)

    lax.fori_loop(1, NLAT, send_row, 0)
    own_rows = pltpu.make_async_copy(send_rows.at[me], rows_out.at[me], sems.at[4])
    own_meta = pltpu.make_async_copy(send_meta.at[me], meta_out.at[me], sems.at[5])
    own_rows.start()
    own_meta.start()
    own_rows.wait()
    own_meta.wait()
    others = pl.ds(0, NDEV - 1)
    pltpu.make_async_copy(send_rows.at[others], send_rows.at[others], sems.at[0]).wait()
    pltpu.make_async_copy(send_meta.at[others], send_meta.at[others], sems.at[2]).wait()
    pltpu.make_async_copy(rows_out.at[others], rows_out.at[others], sems.at[1]).wait()
    pltpu.make_async_copy(meta_out.at[others], meta_out.at[others], sems.at[3]).wait()


def exchange(obs_count, obs_kernel, obs_depart, obs_dest, obs_col):
    vmem = pl.BlockSpec(memory_space=pltpu.VMEM)
    return pl.pallas_call(
        exchange_kernel,
        out_shape=[
            jax.ShapeDtypeStruct((NDEV, CAP, LEV), BF16),
            jax.ShapeDtypeStruct((NDEV, 1, 128), I32),
        ],
        in_specs=[pl.BlockSpec(memory_space=pltpu.SMEM)] + [vmem] * 4,
        out_specs=[vmem, vmem],
        scratch_shapes=[
            pltpu.VMEM((NDEV, CAP, LEV), BF16),
            pltpu.VMEM((NDEV, 1, 128), I32),
            pltpu.VMEM((OBS, LEV), BF16),
            pltpu.SemaphoreType.REGULAR((NLAT,)),
            DMA((6,)),
        ],
        compiler_params=pltpu.CompilerParams(collective_id=0, has_side_effects=True),
        name="exchange",
    )(
        obs_count, obs_kernel, obs_depart.reshape(16, 128),
        obs_dest.reshape(16, 128), obs_col.reshape(16, 128),
    )


def column_kernel(
    rows_ref, meta_ref, field_hbm, mixing_ref, top_ref, frac_ref, thick_ref, courant_hbm, shift_ref, zfrac_ref,
    out_ref, halo_in, next_in, next_halo_in, next_given_in,
    rows_t, cols_hot, row_of, thick_full, forced, given, first, edge, field, mass, weights, halo_sems, next_sems,
    field_sems, courant_sems,
):
    step = pl.program_id(0)
    lat, lon = lax.axis_index("lat"), lax.axis_index("lon")
    west = lax.rem(lon + NLON - 1, NLON)
    east = lax.rem(lon + 1, NLON)
    north = lax.rem(lat + NLAT - 1, NLAT)
    has_north, has_south = lat > 0, lat < NLAT - 1

    def halo_copy(block):
        return pltpu.make_async_remote_copy(
            edge.at[pl.ds(block * 4, 4)], halo_in.at[pl.ds(block * 4, 4)],
            halo_sems.at[0, block], halo_sems.at[1, block], device_id=(lat, west), device_id_type=MESH,
        )

    def next_copy(which):
        source = (given, first, edge.at[0])[which]
        target = (next_given_in, next_in, next_halo_in)[which]
        column = (lon, lon, west)[which]
        return pltpu.make_async_remote_copy(
            source, target, next_sems.at[0, which], next_sems.at[1, which],
            device_id=(north, column), device_id_type=MESH,
        )

    @pl.when(step == 0)
    def _():
        def fetch(row, carry):
            for half in range(2):
                pltpu.make_async_copy(
                    field_hbm.at[:, place(row, half), :], field.at[row, half], field_sems.at[row // 8]
                ).start()
            return carry

        lax.fori_loop(0, ROWS, fetch, 0)
        barrier = pltpu.get_barrier_semaphore()
        south = lax.rem(lat + 1, NLAT)
        for target in (
            (lat, west), (lat, east), (north, lon), (south, lon), (north, west), (south, east)
        ):
            pl.semaphore_signal(barrier, inc=1, device_id=target, device_id_type=MESH)
        first_courant = [
            pltpu.make_async_copy(
                courant_hbm.at[:, place(0, half), :],
                given.at[pl.ds(0, LEV), pl.ds(half * 128, 128)],
                courant_sems.at[half],
            )
            for half in range(2)
        ]
        for copy in first_courant:
            copy.start()
        given[128:136, 0:128] = shift_ref[0:8, :].astype(F32)
        given[128:136, 128:256] = jnp.zeros((8, 128), F32)
        blank = jnp.zeros((LEV - ROWS, 128), F32)
        weights[...] = jnp.transpose(jnp.concatenate([zfrac_ref[...], blank], axis=0))
        cells = jnp.sum(meta_ref[...].reshape(16, 8, 128), axis=1)
        cell_rows = (cells // COLS).astype(F32)
        columns = jnp.transpose((cells % COLS).astype(F32))
        eye = jnp.where(iota((128, 128), 0) == iota((128, 128), 1), 1.0, 0.0).astype(BF16)
        wide = iota((128, COLS), 1).astype(F32)
        for b in range(16):
            row_of[:, b * 128 : b * 128 + 128] = cell_rows[b : b + 1, :]
            span = pl.ds(b * 128, 128)
            cols_hot[span, :] = jnp.where(
                jnp.broadcast_to(columns[:, b : b + 1], (128, COLS)) == wide, 1.0, 0.0
            ).astype(BF16)
            rows_t[:, span] = lax.dot_general(
                eye, rows_ref[span, :], (((1,), (1,)), ((), ())), preferred_element_type=F32
            )
        thick = jnp.transpose(jnp.broadcast_to(thick_ref[...], (128, 128)))
        thick_full[...] = thick
        below = jnp.where(iota((128, 128), 0) <= iota((128, 128), 1), thick, 0.0)
        sums = jnp.broadcast_to(jnp.sum(below, axis=0, keepdims=True), (ROWS, 128))
        for half in range(2):
            span = pl.ds(half * 128, 128)
            mass[:, span] = jnp.take_along_axis(sums, top_ref[:, span] - 1, axis=1, mode="promise_in_bounds")
        pl.semaphore_wait(barrier, 6)
        for copy in first_courant:
            copy.wait()

        @pl.when(has_north)
        def _():
            next_copy(0).start()

    base = (step * 8).astype(F32)
    row_ids = row_of[...]
    pieces = [jnp.where(row_ids == base + float(r), rows_t[...], 0.0).astype(BF16) for r in range(8)]
    forced[...] = jnp.dot(jnp.concatenate(pieces, axis=0), cols_hot[...], preferred_element_type=F32)
    lane = iota((LEV, 128), 1)
    low_lane = (lane[0:64, :] < PACK - 1) | (lane[0:64, :] == 127)
    here = pl.ds(step * 8, 8)
    pltpu.make_async_copy(field.at[here], field.at[here], field_sems.at[step]).wait()
    levels = iota((LEV, 128), 0)

    def one_row(r):
        row = step * 8 + r
        tops, fractions, masses = (ref[pl.ds(row, 1), :] for ref in (top_ref, frac_ref, mass))
        matrix = mixing_ref[r]
        m_hi = matrix.astype(BF16)
        m_lo = (matrix - m_hi.astype(F32)).astype(BF16)
        left = jnp.concatenate([m_hi, m_lo, m_hi], axis=1)
        parts = []
        for half in range(2):
            span = pl.ds(half * 128, 128)
            start = pl.multiple_of(r * 128, 128)
            value = field[row, half] + forced[pl.ds(start, 128), span]
            v_hi = value.astype(BF16)
            v_lo = (value - v_hi.astype(F32)).astype(BF16)
            mixed = jnp.dot(left, jnp.concatenate([v_hi, v_hi, v_lo], axis=0), preferred_element_type=F32)
            cloudy = levels < tops[:, half * 128 : half * 128 + 128]
            total = jnp.sum(jnp.where(cloudy, mixed, 0.0), axis=0, keepdims=True)
            fraction = fractions[:, half * 128 : half * 128 + 128]
            share = fraction * (total / masses[:, half * 128 : half * 128 + 128])
            convected = jnp.where(cloudy, mixed * (1.0 - fraction) + thick_full[...] * share, mixed)
            parts.append(convected)
        weight = jnp.take_along_axis(
            weights[...], jnp.full((LEV, 128), row, I32), axis=1, mode="promise_in_bounds"
        )
        turned = [pltpu.roll(part, 127, 1) for part in parts]
        between = parts[0] + weight * (jnp.where(lane == 127, turned[1], turned[0]) - parts[0])
        out_ref[r, :, 0:128] = between
        out_ref[r, :, 128:256] = parts[1] + weight * (jnp.where(lane == 127, 0.0, turned[1]) - parts[1])
        sent = jnp.where(lane == 127, weight * turned[0], between)
        edge[row] = jnp.where(low_lane, sent[0:64, :], pltpu.roll(sent[64:128, :], PACK, 1)).astype(BF16)

    def rows_of(pair, carry):
        for i in range(UNROLL):
            one_row(pair * UNROLL + i)
        halo_copy(step * 2 + pair).start()
        return carry

    lax.fori_loop(0, 8 // UNROLL, rows_of, 0)

    @pl.when((step == 0) & has_north)
    def _():
        first[...] = out_ref[0]
        next_copy(1).start()
        next_copy(2).start()

    @pl.when(step == 3)
    def _():
        @pl.when(has_north)
        def _():
            for which in range(3):
                next_copy(which).wait_send()

        @pl.when(has_south)
        def _():
            for which in range(3):
                next_copy(which).wait_recv()

        for block in range(ROWS // 4):
            halo_copy(block).wait()


def column_step(rows, meta, field, mixing, top, frac, thick, courant, shift, zfrac):
    whole = lambda *shape: pl.BlockSpec(shape, lambda i: (0,) * len(shape))
    anywhere = pl.BlockSpec(memory_space=pl.ANY)
    return pl.pallas_call(
        column_kernel,
        grid=(4,),
        out_shape=[
            jax.ShapeDtypeStruct((ROWS, LEV, COLS), F32),
            jax.ShapeDtypeStruct((ROWS, 64, 128), BF16),
            jax.ShapeDtypeStruct((LEV, COLS), F32),
            jax.ShapeDtypeStruct((64, 128), BF16),
            jax.ShapeDtypeStruct((LEV + 8, COLS), F32),
        ],
        in_specs=[
            whole(OBS, LEV),
            whole(NDEV, 128),
            anywhere,
            pl.BlockSpec((8, LEV, LEV), lambda i: (i, 0, 0)),
            whole(ROWS, COLS),
            whole(ROWS, COLS),
            whole(1, LEV),
            anywhere,
            whole(ROWS, LEV),
            whole(ROWS, LEV),
        ],
        out_specs=[pl.BlockSpec((8, LEV, COLS), lambda i: (i, 0, 0))] + [anywhere] * 4,
        scratch_shapes=[
            pltpu.VMEM((LEV, OBS), F32),
            pltpu.VMEM((OBS, COLS), BF16),
            pltpu.VMEM((1, OBS), F32),
            pltpu.VMEM((LEV, 128), F32),
            pltpu.VMEM((8 * LEV, COLS), F32),
            pltpu.VMEM((LEV + 8, COLS), F32),
            pltpu.VMEM((LEV, COLS), F32),
            pltpu.VMEM((ROWS, 64, 128), BF16),
            pltpu.VMEM((ROWS, 2, LEV, 128), F32),
            pltpu.VMEM((ROWS, COLS), F32),
            pltpu.VMEM((LEV, 128), F32),
            DMA((2, ROWS // 4)),
            DMA((2, 3)),
            DMA((4,)),
            DMA((2,)),
        ],
        compiler_params=pltpu.CompilerParams(
            vmem_limit_bytes=56 * 1024 * 1024, collective_id=1, has_side_effects=True
        ),
        name="column",
    )(rows, meta, field.reshape(LEV, 64, 128), mixing, top, frac, thick, courant.reshape(LEV, 64, 128), shift, zfrac)


def place(row, half):
    return row // 8 * 16 + half * 8 + row % 8


def transport_kernel(
    conv_hbm, halo_hbm, next_conv_ref, next_halo_ref, next_given_ref, shift_ref, courant_hbm, out_hbm,
    conv, halo, courant, out, shifts, moved, conv_sems, courant_sems, halo_sems, out_sem,
):
    last = lax.axis_index("lat") == NLAT - 1
    groups = ROWS // GROUP

    def conv_copy(group):
        rows = pl.ds(group * GROUP, GROUP)
        return pltpu.make_async_copy(conv_hbm.at[rows], conv.at[rows], conv_sems.at[group])

    def halo_copy(group):
        rows = pl.ds(group * GROUP, GROUP)
        return pltpu.make_async_copy(halo_hbm.at[rows], halo.at[rows], halo_sems.at[group])

    def fetch(group):
        conv_copy(group).start()
        halo_copy(group).start()
        for i in range(GROUP):
            row = group * GROUP + i
            for half in range(2):
                pltpu.make_async_copy(
                    courant_hbm.at[:, place(row, half), :], courant.at[row, half], courant_sems.at[group]
                ).start()

    for ahead in range(AHEAD):
        fetch(groups - 1 - ahead)

    given = jnp.where(last, 0.0, next_given_ref[128:136, :])
    blank = jnp.zeros((LEV - ROWS - 1, 128), F32)
    by_row = jnp.transpose(
        jnp.concatenate([shift_ref[...].astype(F32), given[0:1, 0:128], blank], axis=0)
    )
    column = iota((LEV, 128), 1)
    ones = jnp.ones((128, 128), BF16)
    for row in range(ROWS + 1):
        alone = jnp.where(column == row, by_row, 0.0).astype(BF16)
        shifts[row, :, :] = jnp.dot(alone, ones, preferred_element_type=F32).astype(I32)
    lane = iota((PART, 128), 1)

    def lanes(values, index):
        return jnp.take_along_axis(values, index, axis=1, mode="promise_in_bounds")

    def zonal(first, second, packed, part, row):
        levels = pl.ds(part * PART, PART)
        third = packed[pl.ds(part * PART % 64, PART), :].astype(F32)
        if part * PART >= 64:
            third = pltpu.roll(third, PACK, 1)
        shift = shifts[row, levels, :]
        second = second + jnp.where(lane == 127, third, 0.0)
        index = lane + shift
        wrapped = index & 127
        a = lanes(jnp.where(lane < shift, third, first), wrapped)
        b = lanes(second, wrapped)
        inside = index < 128
        return jnp.where(inside, a, b), jnp.where(inside, b, a)

    for part in range(LEV // PART):
        levels = pl.ds(part * PART, PART)
        both = zonal(next_conv_ref[levels, 0:128], next_conv_ref[levels, 128:256], next_halo_ref, part, ROWS)
        for half in range(2):
            span = pl.ds(half * 128, 128)
            moved[half, levels, :] = jnp.where(last, 0.0, next_given_ref[levels, span] * both[half])
    def step(back, carry):
        group = groups - 1 - back
        rows = pl.ds(group * GROUP, GROUP)

        @pl.when(group >= AHEAD)
        def _():
            fetch(group - AHEAD)

        conv_copy(group).wait()
        halo_copy(group).wait()
        pltpu.make_async_copy(courant.at[rows], courant.at[rows], courant_sems.at[group]).wait()
        for part in range(LEV // PART):
            levels = pl.ds(part * PART, PART)
            coming = [moved[0, levels, :], moved[1, levels, :]]
            for i in reversed(range(GROUP)):
                row = group * GROUP + i
                both = zonal(conv[row, levels, 0:128], conv[row, levels, 128:256], halo.at[row], part, row)
                for half in range(2):
                    leaving = courant[row, half, levels, :] * both[half]
                    out[row, half, levels, :] = both[half] - leaving + coming[half]
                    coming[half] = leaving
            for half in range(2):
                moved[half, levels, :] = coming[half]
        for i in range(GROUP):
            row = group * GROUP + i
            for half in range(2):
                pltpu.make_async_copy(
                    out.at[row, half], out_hbm.at[:, place(row, half), :], out_sem
                ).start()
        return carry

    lax.fori_loop(0, groups, step, 0)
    pltpu.make_async_copy(out, out, out_sem).wait()


def transport(conv, halo, next_conv, next_halo, next_given, shift, courant):
    vmem = pl.BlockSpec(memory_space=pltpu.VMEM)
    anywhere = pl.BlockSpec(memory_space=pl.ANY)
    return pl.pallas_call(
        transport_kernel,
        out_shape=jax.ShapeDtypeStruct((LEV, 64, 128), F32),
        in_specs=[anywhere, anywhere] + [vmem] * 4 + [anywhere],
        out_specs=anywhere,
        scratch_shapes=[
            pltpu.VMEM((ROWS, LEV, COLS), F32),
            pltpu.VMEM((ROWS, 64, 128), BF16),
            pltpu.VMEM((ROWS, 2, LEV, 128), F32),
            pltpu.VMEM((ROWS, 2, LEV, 128), F32),
            pltpu.VMEM((ROWS + 1, LEV, 128), I32),
            pltpu.VMEM((2, LEV, 128), F32),
            DMA((ROWS // GROUP,)),
            DMA((ROWS // GROUP,)),
            DMA((ROWS // GROUP,)),
            DMA,
        ],
        compiler_params=pltpu.CompilerParams(vmem_limit_bytes=60 * 1024 * 1024),
        name="transport",
    )(conv, halo, next_conv, next_halo, next_given, shift, courant.reshape(LEV, 64, 128))


def tiles(value):
    return value.reshape(LEV, 4, 8, 2, 128).transpose(0, 1, 3, 2, 4).reshape(LEV, 4, 16, 128)


def untiles(value):
    return value.reshape(LEV, 4, 2, 8, 128).transpose(0, 1, 3, 2, 4).reshape(LEV, ROWS, COLS)


def shards(
    adjoint_field, mixing_inverse, cloud_top, conv_frac, thickness, zonal_shift, zonal_frac,
    merid_courant, obs_kernel, obs_depart, obs_dest, obs_col, obs_count,
):
    courant = tiles(merid_courant)
    shift, zfrac = zonal_shift.T, zonal_frac.T
    rows, meta = exchange(obs_count, obs_kernel, obs_depart, obs_dest, obs_col)
    conv, halo, next_conv, next_halo, next_given = column_step(
        rows.reshape(OBS, LEV), meta.reshape(NDEV, 128), tiles(adjoint_field), mixing_inverse,
        cloud_top, conv_frac, thickness.reshape(1, LEV), courant, shift, zfrac,
    )
    out = transport(conv, halo, next_conv, next_halo, next_given, shift, courant)
    return untiles(out)


def solution(mesh):
    split = P(None, "lat", "lon")
    both = P(("lat", "lon"))
    return jax.shard_map(
        shards,
        mesh=mesh,
        in_specs=(
            split, P("lat", None, None), P("lat", "lon"), P("lat", "lon"), P(), P(None, "lat"), P(None, "lat"),
            split, P(("lat", "lon"), None), both, both, both, both,
        ),
        out_specs=split,
        check_vma=False,
    )
```

```python
import functools

import jax
import jax.numpy as jnp
from jax import lax
from jax.experimental import pallas as pl
from jax.experimental.pallas import tpu as pltpu
from jax.sharding import PartitionSpec as P

MESH = pl.DeviceIdType.MESH
F32 = jnp.float32
BF16 = jnp.bfloat16
I32 = jnp.int32
DMA = pltpu.SemaphoreType.DMA
NLAT, NLON, NDEV = 8, 16, 128
LEV, ROWS, COLS = 128, 32, 256
OBS, CAP = 2048, 16
PACK = 64
PART = 16
GROUP = 2
AHEAD = 4
UNROLL = 4


def iota(shape, axis):
    return lax.broadcasted_iota(I32, shape, axis)


def exchange_kernel(
    count_ref, kernel_ref, depart_ref, dest_ref, col_ref, rows_out, meta_out,
    send_rows, send_meta, contribution, entered, sems,
):
    lat, lon = lax.axis_index("lat"), lax.axis_index("lon")
    me = lat * NLON + lon
    barrier = pltpu.get_barrier_semaphore()

    def greet(target_of, semaphore, count):
        def body(step, carry):
            pl.semaphore_signal(semaphore, inc=1, device_id=target_of(step), device_id_type=MESH)
            return carry

        lax.fori_loop(1, count, body, 0)

    lon_peer = lambda step: (lat, lax.rem(lon + step, NLON))
    lat_peer = lambda step: (lax.rem(lat + step, NLAT), lon)
    greet(lon_peer, barrier, NLON)
    greet(lat_peer, barrier, NLAT)

    dest = dest_ref[...]
    sub, lane = iota((16, 128), 0), iota((16, 128), 1)
    flat = sub * 128 + lane
    rank = jnp.zeros((16, 128), I32)
    for step in range(1, CAP):
        rolled = pltpu.roll(dest, step, 1)
        before = jnp.where(lane < step, pltpu.roll(rolled, 1, 0), rolled)
        rank = rank + jnp.where((before == dest) & (flat >= step), 1, 0)
    live = flat < count_ref[0]
    slot = jnp.where(live, dest * CAP + rank, -1)
    dest_live = jnp.where(live, dest, -1)
    cells = col_ref[...]
    cell_row = (cells // COLS).astype(F32)
    cell_col = (cells % COLS).astype(F32)

    exact = depart_ref[...]
    high = exact.astype(BF16).astype(F32)
    middle = (exact - high).astype(BF16).astype(F32)
    thirds = [high, middle, exact - high - middle, jnp.zeros((80, 128), F32)]
    depart_t = jnp.transpose(jnp.concatenate(thirds, axis=0))
    place_of = iota((128, 128), 1) % 16
    every = jnp.ones((128, 128), BF16)
    for block in range(16):
        span = pl.ds(block * 128, 128)
        alone = jnp.where(place_of == block, depart_t, 0.0).astype(BF16)
        spread = jnp.dot(alone, every, preferred_element_type=F32)
        contribution[span, :] = (kernel_ref[span, :].astype(F32) * spread).astype(BF16)

    pl.semaphore_wait(barrier, NLON + NLAT - 2)
    greet(lat_peer, entered.at[lat], NLAT)

    big_sub = iota((128, 128), 0)
    mine = (big_sub // CAP) == lax.rem(me, 8)
    meta = jnp.zeros((128, 128), F32)
    nt = (((1,), (1,)), ((), ()))
    for block in range(16):
        owner = jnp.where(dest_live[block : block + 1, :] == big_sub, 1.0, 0.0).astype(BF16)
        place = (rank[block : block + 1, :] == big_sub % CAP) & mine
        row_part = jnp.where(place, cell_row[block : block + 1, :], 0.0).astype(BF16)
        col_part = jnp.where(place, cell_col[block : block + 1, :], 0.0).astype(BF16)
        meta = meta + float(COLS) * lax.dot_general(owner, row_part, nt, preferred_element_type=F32)
        meta = meta + lax.dot_general(owner, col_part, nt, preferred_element_type=F32)
    meta = meta.astype(I32)
    for dst in range(NDEV):
        send_meta[dst, :, :] = meta[dst : dst + 1, :]

    for out_block in range(16):
        width = (out_block + 1) * 128
        wanted = big_sub + out_block * 128
        hits = [
            jnp.where(slot[block : block + 1, :] == wanted, 1.0, 0.0).astype(BF16)
            for block in range(out_block + 1)
        ]
        total = jnp.dot(jnp.concatenate(hits, axis=1), contribution[0:width, :], preferred_element_type=F32)
        send_rows[pl.ds(out_block * 8, 8), :, :] = total.astype(BF16).reshape(8, CAP, LEV)

    def send_to(to_lat, to_lon):
        target = to_lat * NLON + to_lon
        pltpu.make_async_remote_copy(
            send_rows.at[target], rows_out.at[me], sems.at[0], sems.at[1],
            device_id=(to_lat, to_lon), device_id_type=MESH,
        ).start()
        pltpu.make_async_remote_copy(
            send_meta.at[target], meta_out.at[me], sems.at[2], sems.at[3],
            device_id=(to_lat, to_lon), device_id_type=MESH,
        ).start()

    def send_near(step, carry):
        send_to(lat, lax.rem(lon + step, NLON))
        return carry

    lax.fori_loop(1, NLON, send_near, 0, unroll=5)

    def send_row(step, carry):
        to_lat = lax.rem(lat + step, NLAT)
        pl.semaphore_wait(entered.at[to_lat], 1)

        def send_far(turn, inner):
            send_to(to_lat, lax.rem(lon + turn, NLON))
            return inner

        return lax.fori_loop(0, NLON, send_far, carry, unroll=8)

    lax.fori_loop(1, NLAT, send_row, 0)
    own_rows = pltpu.make_async_copy(send_rows.at[me], rows_out.at[me], sems.at[4])
    own_meta = pltpu.make_async_copy(send_meta.at[me], meta_out.at[me], sems.at[5])
    own_rows.start()
    own_meta.start()
    own_rows.wait()
    own_meta.wait()
    others = pl.ds(0, NDEV - 1)
    pltpu.make_async_copy(send_rows.at[others], send_rows.at[others], sems.at[0]).wait()
    pltpu.make_async_copy(send_meta.at[others], send_meta.at[others], sems.at[2]).wait()
    pltpu.make_async_copy(rows_out.at[others], rows_out.at[others], sems.at[1]).wait()
    pltpu.make_async_copy(meta_out.at[others], meta_out.at[others], sems.at[3]).wait()


def exchange(obs_count, obs_kernel, obs_depart, obs_dest, obs_col):
    vmem = pl.BlockSpec(memory_space=pltpu.VMEM)
    return pl.pallas_call(
        exchange_kernel,
        out_shape=[
            jax.ShapeDtypeStruct((NDEV, CAP, LEV), BF16),
            jax.ShapeDtypeStruct((NDEV, 1, 128), I32),
        ],
        in_specs=[pl.BlockSpec(memory_space=pltpu.SMEM)] + [vmem] * 4,
        out_specs=[vmem, vmem],
        scratch_shapes=[
            pltpu.VMEM((NDEV, CAP, LEV), BF16),
            pltpu.VMEM((NDEV, 1, 128), I32),
            pltpu.VMEM((OBS, LEV), BF16),
            pltpu.SemaphoreType.REGULAR((NLAT,)),
            DMA((6,)),
        ],
        compiler_params=pltpu.CompilerParams(collective_id=0, has_side_effects=True),
        name="exchange",
    )(
        obs_count, obs_kernel, obs_depart.reshape(16, 128),
        obs_dest.reshape(16, 128), obs_col.reshape(16, 128),
    )


def column_kernel(
    rows_ref, meta_ref, field_hbm, mixing_ref, top_ref, frac_ref, thick_ref, courant_hbm, shift_ref, zfrac_ref,
    out_ref, halo_in, next_in, next_halo_in, next_given_in,
    rows_t, cols_hot, row_of, thick_full, forced, given, first, edge, field, mass, weights, halo_sems, next_sems,
    field_sems, courant_sems,
):
    step = pl.program_id(0)
    lat, lon = lax.axis_index("lat"), lax.axis_index("lon")
    west = lax.rem(lon + NLON - 1, NLON)
    east = lax.rem(lon + 1, NLON)
    north = lax.rem(lat + NLAT - 1, NLAT)
    has_north, has_south = lat > 0, lat < NLAT - 1

    def halo_copy(block):
        return pltpu.make_async_remote_copy(
            edge.at[pl.ds(block * 4, 4)], halo_in.at[pl.ds(block * 4, 4)],
            halo_sems.at[0, block], halo_sems.at[1, block], device_id=(lat, west), device_id_type=MESH,
        )

    def next_copy(which):
        source = (given, first, edge.at[0])[which]
        target = (next_given_in, next_in, next_halo_in)[which]
        column = (lon, lon, west)[which]
        return pltpu.make_async_remote_copy(
            source, target, next_sems.at[0, which], next_sems.at[1, which],
            device_id=(north, column), device_id_type=MESH,
        )

    @pl.when(step == 0)
    def _():
        def fetch(row, carry):
            for half in range(2):
                pltpu.make_async_copy(
                    field_hbm.at[:, place(row, half), :], field.at[row, half], field_sems.at[row // 8]
                ).start()
            return carry

        lax.fori_loop(0, ROWS, fetch, 0)
        barrier = pltpu.get_barrier_semaphore()
        south = lax.rem(lat + 1, NLAT)
        for target in (
            (lat, west), (lat, east), (north, lon), (south, lon), (north, west), (south, east)
        ):
            pl.semaphore_signal(barrier, inc=1, device_id=target, device_id_type=MESH)
        first_courant = [
            pltpu.make_async_copy(
                courant_hbm.at[:, place(0, half), :],
                given.at[pl.ds(0, LEV), pl.ds(half * 128, 128)],
                courant_sems.at[half],
            )
            for half in range(2)
        ]
        for copy in first_courant:
            copy.start()
        given[128:136, 0:128] = shift_ref[0:8, :].astype(F32)
        given[128:136, 128:256] = jnp.zeros((8, 128), F32)
        blank = jnp.zeros((LEV - ROWS, 128), F32)
        weights[...] = jnp.transpose(jnp.concatenate([zfrac_ref[...], blank], axis=0))
        cells = jnp.sum(meta_ref[...].reshape(16, 8, 128), axis=1)
        cell_rows = (cells // COLS).astype(F32)
        columns = jnp.transpose((cells % COLS).astype(F32))
        eye = jnp.where(iota((128, 128), 0) == iota((128, 128), 1), 1.0, 0.0).astype(BF16)
        wide = iota((128, COLS), 1).astype(F32)
        columns = jnp.concatenate([columns, jnp.zeros((128, 112), F32)], axis=1)
        place_lane = iota((128, 128), 1)
        every = jnp.ones((128, COLS), BF16)
        for b in range(16):
            row_of[:, b * 128 : b * 128 + 128] = cell_rows[b : b + 1, :]
            span = pl.ds(b * 128, 128)
            alone = jnp.where(place_lane == b, columns, 0.0).astype(BF16)
            spread = jnp.dot(alone, every, preferred_element_type=F32)
            cols_hot[span, :] = jnp.where(spread == wide, 1.0, 0.0).astype(BF16)
            rows_t[:, span] = lax.dot_general(
                eye, rows_ref[span, :], (((1,), (1,)), ((), ())), preferred_element_type=F32
            )
        thick = jnp.transpose(jnp.broadcast_to(thick_ref[...], (128, 128)))
        thick_full[...] = thick
        below = jnp.where(iota((128, 128), 0) <= iota((128, 128), 1), thick, 0.0)
        sums = jnp.broadcast_to(jnp.sum(below, axis=0, keepdims=True), (ROWS, 128))
        for half in range(2):
            span = pl.ds(half * 128, 128)
            mass[:, span] = jnp.take_along_axis(sums, top_ref[:, span] - 1, axis=1, mode="promise_in_bounds")
        pl.semaphore_wait(barrier, 6)
        for copy in first_courant:
            copy.wait()

        @pl.when(has_north)
        def _():
            next_copy(0).start()

    base = (step * 8).astype(F32)
    row_ids = row_of[...]
    pieces = [jnp.where(row_ids == base + float(r), rows_t[...], 0.0).astype(BF16) for r in range(8)]
    forced[...] = jnp.dot(jnp.concatenate(pieces, axis=0), cols_hot[...], preferred_element_type=F32)
    lane = iota((LEV, 128), 1)
    low_lane = (lane[0:64, :] < PACK - 1) | (lane[0:64, :] == 127)
    here = pl.ds(step * 8, 8)
    pltpu.make_async_copy(field.at[here], field.at[here], field_sems.at[step]).wait()
    levels = iota((LEV, 128), 0)

    def one_row(r):
        row = step * 8 + r
        tops, fractions, masses = (ref[pl.ds(row, 1), :] for ref in (top_ref, frac_ref, mass))
        matrix = mixing_ref[r]
        m_hi = matrix.astype(BF16)
        m_lo = (matrix - m_hi.astype(F32)).astype(BF16)
        left = jnp.concatenate([m_hi, m_lo, m_hi], axis=1)
        parts = []
        for half in range(2):
            span = pl.ds(half * 128, 128)
            start = pl.multiple_of(r * 128, 128)
            value = field[row, half] + forced[pl.ds(start, 128), span]
            v_hi = value.astype(BF16)
            v_lo = (value - v_hi.astype(F32)).astype(BF16)
            mixed = jnp.dot(left, jnp.concatenate([v_hi, v_hi, v_lo], axis=0), preferred_element_type=F32)
            cloudy = levels < tops[:, half * 128 : half * 128 + 128]
            total = jnp.sum(jnp.where(cloudy, mixed, 0.0), axis=0, keepdims=True)
            fraction = fractions[:, half * 128 : half * 128 + 128]
            share = fraction * (total / masses[:, half * 128 : half * 128 + 128])
            convected = jnp.where(cloudy, mixed * (1.0 - fraction) + thick_full[...] * share, mixed)
            parts.append(convected)
        weight = jnp.take_along_axis(
            weights[...], jnp.full((LEV, 128), row, I32), axis=1, mode="promise_in_bounds"
        )
        turned = [pltpu.roll(part, 127, 1) for part in parts]
        between = parts[0] + weight * (jnp.where(lane == 127, turned[1], turned[0]) - parts[0])
        out_ref[r, :, 0:128] = between
        out_ref[r, :, 128:256] = parts[1] + weight * (jnp.where(lane == 127, 0.0, turned[1]) - parts[1])
        sent = jnp.where(lane == 127, weight * turned[0], between)
        edge[row] = jnp.where(low_lane, sent[0:64, :], pltpu.roll(sent[64:128, :], PACK, 1)).astype(BF16)

    def rows_of(pair, carry):
        for i in range(UNROLL):
            one_row(pair * UNROLL + i)
        halo_copy(step * 2 + pair).start()
        return carry

    lax.fori_loop(0, 8 // UNROLL, rows_of, 0)

    @pl.when((step == 0) & has_north)
    def _():
        first[...] = out_ref[0]
        next_copy(1).start()
        next_copy(2).start()

    @pl.when(step == 3)
    def _():
        @pl.when(has_north)
        def _():
            for which in range(3):
                next_copy(which).wait_send()

        @pl.when(has_south)
        def _():
            for which in range(3):
                next_copy(which).wait_recv()

        for block in range(ROWS // 4):
            halo_copy(block).wait()


def column_step(rows, meta, field, mixing, top, frac, thick, courant, shift, zfrac):
    whole = lambda *shape: pl.BlockSpec(shape, lambda i: (0,) * len(shape))
    anywhere = pl.BlockSpec(memory_space=pl.ANY)
    return pl.pallas_call(
        column_kernel,
        grid=(4,),
        out_shape=[
            jax.ShapeDtypeStruct((ROWS, LEV, COLS), F32),
            jax.ShapeDtypeStruct((ROWS, 64, 128), BF16),
            jax.ShapeDtypeStruct((LEV, COLS), F32),
            jax.ShapeDtypeStruct((64, 128), BF16),
            jax.ShapeDtypeStruct((LEV + 8, COLS), F32),
        ],
        in_specs=[
            whole(OBS, LEV),
            whole(NDEV, 128),
            anywhere,
            pl.BlockSpec((8, LEV, LEV), lambda i: (i, 0, 0)),
            whole(ROWS, COLS),
            whole(ROWS, COLS),
            whole(1, LEV),
            anywhere,
            whole(ROWS, LEV),
            whole(ROWS, LEV),
        ],
        out_specs=[pl.BlockSpec((8, LEV, COLS), lambda i: (i, 0, 0))] + [anywhere] * 4,
        scratch_shapes=[
            pltpu.VMEM((LEV, OBS), F32),
            pltpu.VMEM((OBS, COLS), BF16),
            pltpu.VMEM((1, OBS), F32),
            pltpu.VMEM((LEV, 128), F32),
            pltpu.VMEM((8 * LEV, COLS), F32),
            pltpu.VMEM((LEV + 8, COLS), F32),
            pltpu.VMEM((LEV, COLS), F32),
            pltpu.VMEM((ROWS, 64, 128), BF16),
            pltpu.VMEM((ROWS, 2, LEV, 128), F32),
            pltpu.VMEM((ROWS, COLS), F32),
            pltpu.VMEM((LEV, 128), F32),
            DMA((2, ROWS // 4)),
            DMA((2, 3)),
            DMA((4,)),
            DMA((2,)),
        ],
        compiler_params=pltpu.CompilerParams(
            vmem_limit_bytes=56 * 1024 * 1024, collective_id=1, has_side_effects=True
        ),
        name="column",
    )(rows, meta, field.reshape(LEV, 64, 128), mixing, top, frac, thick, courant.reshape(LEV, 64, 128), shift, zfrac)


def place(row, half):
    return row // 8 * 16 + half * 8 + row % 8


def transport_kernel(
    conv_hbm, halo_hbm, next_conv_ref, next_halo_ref, next_given_ref, shift_ref, courant_hbm, out_hbm,
    conv, halo, courant, out, shifts, moved, conv_sems, courant_sems, halo_sems, out_sem,
):
    last = lax.axis_index("lat") == NLAT - 1
    groups = ROWS // GROUP

    def conv_copy(group):
        rows = pl.ds(group * GROUP, GROUP)
        return pltpu.make_async_copy(conv_hbm.at[rows], conv.at[rows], conv_sems.at[group])

    def halo_copy(group):
        rows = pl.ds(group * GROUP, GROUP)
        return pltpu.make_async_copy(halo_hbm.at[rows], halo.at[rows], halo_sems.at[group])

    def fetch(group):
        conv_copy(group).start()
        halo_copy(group).start()
        for i in range(GROUP):
            row = group * GROUP + i
            for half in range(2):
                pltpu.make_async_copy(
                    courant_hbm.at[:, place(row, half), :], courant.at[row, half], courant_sems.at[group]
                ).start()

    for ahead in range(AHEAD):
        fetch(groups - 1 - ahead)

    given = jnp.where(last, 0.0, next_given_ref[128:136, :])
    blank = jnp.zeros((LEV - ROWS - 1, 128), F32)
    by_row = jnp.transpose(
        jnp.concatenate([shift_ref[...].astype(F32), given[0:1, 0:128], blank], axis=0)
    )
    column = iota((LEV, 128), 1)
    ones = jnp.ones((128, 128), BF16)
    for row in range(ROWS + 1):
        alone = jnp.where(column == row, by_row, 0.0).astype(BF16)
        shifts[row, :, :] = jnp.dot(alone, ones, preferred_element_type=F32).astype(I32)
    lane = iota((PART, 128), 1)

    def lanes(values, index):
        return jnp.take_along_axis(values, index, axis=1, mode="promise_in_bounds")

    def zonal(first, second, packed, part, row):
        levels = pl.ds(part * PART, PART)
        third = packed[pl.ds(part * PART % 64, PART), :].astype(F32)
        if part * PART >= 64:
            third = pltpu.roll(third, PACK, 1)
        shift = shifts[row, levels, :]
        second = second + jnp.where(lane == 127, third, 0.0)
        index = lane + shift
        wrapped = index & 127
        a = lanes(jnp.where(lane < shift, third, first), wrapped)
        b = lanes(second, wrapped)
        inside = index < 128
        return jnp.where(inside, a, b), jnp.where(inside, b, a)

    for part in range(LEV // PART):
        levels = pl.ds(part * PART, PART)
        both = zonal(next_conv_ref[levels, 0:128], next_conv_ref[levels, 128:256], next_halo_ref, part, ROWS)
        for half in range(2):
            span = pl.ds(half * 128, 128)
            moved[half, levels, :] = jnp.where(last, 0.0, next_given_ref[levels, span] * both[half])
    def step(back, carry):
        group = groups - 1 - back
        rows = pl.ds(group * GROUP, GROUP)

        @pl.when(group >= AHEAD)
        def _():
            fetch(group - AHEAD)

        conv_copy(group).wait()
        halo_copy(group).wait()
        pltpu.make_async_copy(courant.at[rows], courant.at[rows], courant_sems.at[group]).wait()
        for part in range(LEV // PART):
            levels = pl.ds(part * PART, PART)
            coming = [moved[0, levels, :], moved[1, levels, :]]
            for i in reversed(range(GROUP)):
                row = group * GROUP + i
                both = zonal(conv[row, levels, 0:128], conv[row, levels, 128:256], halo.at[row], part, row)
                for half in range(2):
                    leaving = courant[row, half, levels, :] * both[half]
                    out[row, half, levels, :] = both[half] - leaving + coming[half]
                    coming[half] = leaving
            for half in range(2):
                moved[half, levels, :] = coming[half]
        for i in range(GROUP):
            row = group * GROUP + i
            for half in range(2):
                pltpu.make_async_copy(
                    out.at[row, half], out_hbm.at[:, place(row, half), :], out_sem
                ).start()
        return carry

    lax.fori_loop(0, groups, step, 0)
    pltpu.make_async_copy(out, out, out_sem).wait()


def transport(conv, halo, next_conv, next_halo, next_given, shift, courant):
    vmem = pl.BlockSpec(memory_space=pltpu.VMEM)
    anywhere = pl.BlockSpec(memory_space=pl.ANY)
    return pl.pallas_call(
        transport_kernel,
        out_shape=jax.ShapeDtypeStruct((LEV, 64, 128), F32),
        in_specs=[anywhere, anywhere] + [vmem] * 4 + [anywhere],
        out_specs=anywhere,
        scratch_shapes=[
            pltpu.VMEM((ROWS, LEV, COLS), F32),
            pltpu.VMEM((ROWS, 64, 128), BF16),
            pltpu.VMEM((ROWS, 2, LEV, 128), F32),
            pltpu.VMEM((ROWS, 2, LEV, 128), F32),
            pltpu.VMEM((ROWS + 1, LEV, 128), I32),
            pltpu.VMEM((2, LEV, 128), F32),
            DMA((ROWS // GROUP,)),
            DMA((ROWS // GROUP,)),
            DMA((ROWS // GROUP,)),
            DMA,
        ],
        compiler_params=pltpu.CompilerParams(vmem_limit_bytes=60 * 1024 * 1024),
        name="transport",
    )(conv, halo, next_conv, next_halo, next_given, shift, courant.reshape(LEV, 64, 128))


def tiles(value):
    return value.reshape(LEV, 4, 8, 2, 128).transpose(0, 1, 3, 2, 4).reshape(LEV, 4, 16, 128)


def untiles(value):
    return value.reshape(LEV, 4, 2, 8, 128).transpose(0, 1, 3, 2, 4).reshape(LEV, ROWS, COLS)


def shards(
    adjoint_field, mixing_inverse, cloud_top, conv_frac, thickness, zonal_shift, zonal_frac,
    merid_courant, obs_kernel, obs_depart, obs_dest, obs_col, obs_count,
):
    courant = tiles(merid_courant)
    shift, zfrac = zonal_shift.T, zonal_frac.T
    rows, meta = exchange(obs_count, obs_kernel, obs_depart, obs_dest, obs_col)
    conv, halo, next_conv, next_halo, next_given = column_step(
        rows.reshape(OBS, LEV), meta.reshape(NDEV, 128), tiles(adjoint_field), mixing_inverse,
        cloud_top, conv_frac, thickness.reshape(1, LEV), courant, shift, zfrac,
    )
    out = transport(conv, halo, next_conv, next_halo, next_given, shift, courant)
    return untiles(out)


def solution(mesh):
    split = P(None, "lat", "lon")
    both = P(("lat", "lon"))
    return jax.shard_map(
        shards,
        mesh=mesh,
        in_specs=(
            split, P("lat", None, None), P("lat", "lon"), P("lat", "lon"), P(), P(None, "lat"), P(None, "lat"),
            split, P(("lat", "lon"), None), both, both, both, both,
        ),
        out_specs=split,
        check_vma=False,
    )
```

```python
import functools

import jax
import jax.numpy as jnp
from jax import lax
from jax.experimental import pallas as pl
from jax.experimental.pallas import tpu as pltpu
from jax.sharding import PartitionSpec as P

MESH = pl.DeviceIdType.MESH
F32 = jnp.float32
BF16 = jnp.bfloat16
I32 = jnp.int32
DMA = pltpu.SemaphoreType.DMA
NLAT, NLON, NDEV = 8, 16, 128
LEV, ROWS, COLS = 128, 32, 256
OBS, CAP = 2048, 16
PACK = 64
PART = 16
GROUP = 2
AHEAD = 6
UNROLL = 4


def iota(shape, axis):
    return lax.broadcasted_iota(I32, shape, axis)


def exchange_kernel(
    count_ref, kernel_ref, depart_ref, dest_ref, col_ref, rows_out, meta_out,
    send_rows, send_meta, contribution, entered, sems,
):
    lat, lon = lax.axis_index("lat"), lax.axis_index("lon")
    me = lat * NLON + lon
    barrier = pltpu.get_barrier_semaphore()

    def greet(target_of, semaphore, count):
        def body(step, carry):
            pl.semaphore_signal(semaphore, inc=1, device_id=target_of(step), device_id_type=MESH)
            return carry

        lax.fori_loop(1, count, body, 0)

    lon_peer = lambda step: (lat, lax.rem(lon + step, NLON))
    lat_peer = lambda step: (lax.rem(lat + step, NLAT), lon)
    greet(lon_peer, barrier, NLON)
    greet(lat_peer, barrier, NLAT)

    dest = dest_ref[...]
    sub, lane = iota((16, 128), 0), iota((16, 128), 1)
    flat = sub * 128 + lane
    rank = jnp.zeros((16, 128), I32)
    for step in range(1, CAP):
        rolled = pltpu.roll(dest, step, 1)
        before = jnp.where(lane < step, pltpu.roll(rolled, 1, 0), rolled)
        rank = rank + jnp.where((before == dest) & (flat >= step), 1, 0)
    live = flat < count_ref[0]
    slot = jnp.where(live, dest * CAP + rank, -1)
    dest_live = jnp.where(live, dest, -1)
    cells = col_ref[...]
    cell_row = (cells // COLS).astype(F32)
    cell_col = (cells % COLS).astype(F32)

    exact = depart_ref[...]
    high = exact.astype(BF16).astype(F32)
    middle = (exact - high).astype(BF16).astype(F32)
    thirds = [high, middle, exact - high - middle, jnp.zeros((80, 128), F32)]
    depart_t = jnp.transpose(jnp.concatenate(thirds, axis=0))
    place_of = iota((128, 128), 1) % 16
    every = jnp.ones((128, 128), BF16)
    for block in range(16):
        span = pl.ds(block * 128, 128)
        alone = jnp.where(place_of == block, depart_t, 0.0).astype(BF16)
        spread = jnp.dot(alone, every, preferred_element_type=F32)
        contribution[span, :] = (kernel_ref[span, :].astype(F32) * spread).astype(BF16)

    pl.semaphore_wait(barrier, NLON + NLAT - 2)
    greet(lat_peer, entered.at[lat], NLAT)

    big_sub = iota((128, 128), 0)
    mine = (big_sub // CAP) == lax.rem(me, 8)
    meta = jnp.zeros((128, 128), F32)
    nt = (((1,), (1,)), ((), ()))
    for block in range(16):
        owner = jnp.where(dest_live[block : block + 1, :] == big_sub, 1.0, 0.0).astype(BF16)
        place = (rank[block : block + 1, :] == big_sub % CAP) & mine
        row_part = jnp.where(place, cell_row[block : block + 1, :], 0.0).astype(BF16)
        col_part = jnp.where(place, cell_col[block : block + 1, :], 0.0).astype(BF16)
        meta = meta + float(COLS) * lax.dot_general(owner, row_part, nt, preferred_element_type=F32)
        meta = meta + lax.dot_general(owner, col_part, nt, preferred_element_type=F32)
    meta = meta.astype(I32)
    for dst in range(NDEV):
        send_meta[dst, :, :] = meta[dst : dst + 1, :]

    for out_block in range(16):
        width = (out_block + 1) * 128
        wanted = big_sub + out_block * 128
        hits = [
            jnp.where(slot[block : block + 1, :] == wanted, 1.0, 0.0).astype(BF16)
            for block in range(out_block + 1)
        ]
        total = jnp.dot(jnp.concatenate(hits, axis=1), contribution[0:width, :], preferred_element_type=F32)
        send_rows[pl.ds(out_block * 8, 8), :, :] = total.astype(BF16).reshape(8, CAP, LEV)

    def send_to(to_lat, to_lon):
        target = to_lat * NLON + to_lon
        pltpu.make_async_remote_copy(
            send_rows.at[target], rows_out.at[me], sems.at[0], sems.at[1],
            device_id=(to_lat, to_lon), device_id_type=MESH,
        ).start()
        pltpu.make_async_remote_copy(
            send_meta.at[target], meta_out.at[me], sems.at[2], sems.at[3],
            device_id=(to_lat, to_lon), device_id_type=MESH,
        ).start()

    def send_near(step, carry):
        send_to(lat, lax.rem(lon + step, NLON))
        return carry

    lax.fori_loop(1, NLON, send_near, 0, unroll=5)

    def send_row(step, carry):
        to_lat = lax.rem(lat + step, NLAT)
        pl.semaphore_wait(entered.at[to_lat], 1)

        def send_far(turn, inner):
            send_to(to_lat, lax.rem(lon + turn, NLON))
            return inner

        return lax.fori_loop(0, NLON, send_far, carry, unroll=8)

    lax.fori_loop(1, NLAT, send_row, 0)
    own_rows = pltpu.make_async_copy(send_rows.at[me], rows_out.at[me], sems.at[4])
    own_meta = pltpu.make_async_copy(send_meta.at[me], meta_out.at[me], sems.at[5])
    own_rows.start()
    own_meta.start()
    own_rows.wait()
    own_meta.wait()
    others = pl.ds(0, NDEV - 1)
    pltpu.make_async_copy(send_rows.at[others], send_rows.at[others], sems.at[0]).wait()
    pltpu.make_async_copy(send_meta.at[others], send_meta.at[others], sems.at[2]).wait()
    pltpu.make_async_copy(rows_out.at[others], rows_out.at[others], sems.at[1]).wait()
    pltpu.make_async_copy(meta_out.at[others], meta_out.at[others], sems.at[3]).wait()


def exchange(obs_count, obs_kernel, obs_depart, obs_dest, obs_col):
    vmem = pl.BlockSpec(memory_space=pltpu.VMEM)
    return pl.pallas_call(
        exchange_kernel,
        out_shape=[
            jax.ShapeDtypeStruct((NDEV, CAP, LEV), BF16),
            jax.ShapeDtypeStruct((NDEV, 1, 128), I32),
        ],
        in_specs=[pl.BlockSpec(memory_space=pltpu.SMEM)] + [vmem] * 4,
        out_specs=[vmem, vmem],
        scratch_shapes=[
            pltpu.VMEM((NDEV, CAP, LEV), BF16),
            pltpu.VMEM((NDEV, 1, 128), I32),
            pltpu.VMEM((OBS, LEV), BF16),
            pltpu.SemaphoreType.REGULAR((NLAT,)),
            DMA((6,)),
        ],
        compiler_params=pltpu.CompilerParams(collective_id=0, has_side_effects=True),
        name="exchange",
    )(
        obs_count, obs_kernel, obs_depart.reshape(16, 128),
        obs_dest.reshape(16, 128), obs_col.reshape(16, 128),
    )


def column_kernel(
    rows_ref, meta_ref, field_hbm, mixing_ref, top_ref, frac_ref, thick_ref, courant_hbm, shift_ref, zfrac_ref,
    out_ref, halo_in, next_in, next_halo_in, next_given_in,
    rows_t, cols_hot, row_of, thick_full, forced, given, first, edge, field, mass, weights, halo_sems, next_sems,
    field_sems, courant_sems,
):
    step = pl.program_id(0)
    lat, lon = lax.axis_index("lat"), lax.axis_index("lon")
    west = lax.rem(lon + NLON - 1, NLON)
    east = lax.rem(lon + 1, NLON)
    north = lax.rem(lat + NLAT - 1, NLAT)
    has_north, has_south = lat > 0, lat < NLAT - 1

    def halo_copy(block):
        return pltpu.make_async_remote_copy(
            edge.at[pl.ds(block * 4, 4)], halo_in.at[pl.ds(block * 4, 4)],
            halo_sems.at[0, block], halo_sems.at[1, block], device_id=(lat, west), device_id_type=MESH,
        )

    def next_copy(which):
        source = (given, first, edge.at[0])[which]
        target = (next_given_in, next_in, next_halo_in)[which]
        column = (lon, lon, west)[which]
        return pltpu.make_async_remote_copy(
            source, target, next_sems.at[0, which], next_sems.at[1, which],
            device_id=(north, column), device_id_type=MESH,
        )

    @pl.when(step == 0)
    def _():
        def fetch(row, carry):
            for half in range(2):
                pltpu.make_async_copy(
                    field_hbm.at[:, place(row, half), :], field.at[row, half], field_sems.at[row // 8]
                ).start()
            return carry

        lax.fori_loop(0, ROWS, fetch, 0)
        barrier = pltpu.get_barrier_semaphore()
        south = lax.rem(lat + 1, NLAT)
        for target in (
            (lat, west), (lat, east), (north, lon), (south, lon), (north, west), (south, east)
        ):
            pl.semaphore_signal(barrier, inc=1, device_id=target, device_id_type=MESH)
        first_courant = [
            pltpu.make_async_copy(
                courant_hbm.at[:, place(0, half), :],
                given.at[pl.ds(0, LEV), pl.ds(half * 128, 128)],
                courant_sems.at[half],
            )
            for half in range(2)
        ]
        for copy in first_courant:
            copy.start()
        given[128:136, 0:128] = shift_ref[0:8, :].astype(F32)
        given[128:136, 128:256] = jnp.zeros((8, 128), F32)
        blank = jnp.zeros((LEV - ROWS, 128), F32)
        weights[...] = jnp.transpose(jnp.concatenate([zfrac_ref[...], blank], axis=0))
        cells = jnp.sum(meta_ref[...].reshape(16, 8, 128), axis=1)
        cell_rows = (cells // COLS).astype(F32)
        columns = jnp.transpose((cells % COLS).astype(F32))
        eye = jnp.where(iota((128, 128), 0) == iota((128, 128), 1), 1.0, 0.0).astype(BF16)
        wide = iota((128, COLS), 1).astype(F32)
        columns = jnp.concatenate([columns, jnp.zeros((128, 112), F32)], axis=1)
        place_lane = iota((128, 128), 1)
        every = jnp.ones((128, COLS), BF16)
        for b in range(16):
            row_of[:, b * 128 : b * 128 + 128] = cell_rows[b : b + 1, :]
            span = pl.ds(b * 128, 128)
            alone = jnp.where(place_lane == b, columns, 0.0).astype(BF16)
            spread = jnp.dot(alone, every, preferred_element_type=F32)
            cols_hot[span, :] = jnp.where(spread == wide, 1.0, 0.0).astype(BF16)
            rows_t[:, span] = lax.dot_general(
                eye, rows_ref[span, :], (((1,), (1,)), ((), ())), preferred_element_type=F32
            )
        thick = jnp.transpose(jnp.broadcast_to(thick_ref[...], (128, 128)))
        thick_full[...] = thick
        below = jnp.where(iota((128, 128), 0) <= iota((128, 128), 1), thick, 0.0)
        sums = jnp.broadcast_to(jnp.sum(below, axis=0, keepdims=True), (ROWS, 128))
        for half in range(2):
            span = pl.ds(half * 128, 128)
            mass[:, span] = jnp.take_along_axis(sums, top_ref[:, span] - 1, axis=1, mode="promise_in_bounds")
        pl.semaphore_wait(barrier, 6)
        for copy in first_courant:
            copy.wait()

        @pl.when(has_north)
        def _():
            next_copy(0).start()

    base = (step * 8).astype(F32)
    row_ids = row_of[...]
    pieces = [jnp.where(row_ids == base + float(r), rows_t[...], 0.0).astype(BF16) for r in range(8)]
    forced[...] = jnp.dot(jnp.concatenate(pieces, axis=0), cols_hot[...], preferred_element_type=F32)
    lane = iota((LEV, 128), 1)
    low_lane = (lane[0:64, :] < PACK - 1) | (lane[0:64, :] == 127)
    here = pl.ds(step * 8, 8)
    pltpu.make_async_copy(field.at[here], field.at[here], field_sems.at[step]).wait()
    levels = iota((LEV, 128), 0)

    def one_row(r):
        row = step * 8 + r
        tops, fractions, masses = (ref[pl.ds(row, 1), :] for ref in (top_ref, frac_ref, mass))
        matrix = mixing_ref[r]
        m_hi = matrix.astype(BF16)
        m_lo = (matrix - m_hi.astype(F32)).astype(BF16)
        left = jnp.concatenate([m_hi, m_lo, m_hi], axis=1)
        parts = []
        for half in range(2):
            span = pl.ds(half * 128, 128)
            start = pl.multiple_of(r * 128, 128)
            value = field[row, half] + forced[pl.ds(start, 128), span]
            v_hi = value.astype(BF16)
            v_lo = (value - v_hi.astype(F32)).astype(BF16)
            mixed = jnp.dot(left, jnp.concatenate([v_hi, v_hi, v_lo], axis=0), preferred_element_type=F32)
            cloudy = levels < tops[:, half * 128 : half * 128 + 128]
            total = jnp.sum(jnp.where(cloudy, mixed, 0.0), axis=0, keepdims=True)
            fraction = fractions[:, half * 128 : half * 128 + 128]
            share = fraction * (total / masses[:, half * 128 : half * 128 + 128])
            convected = jnp.where(cloudy, mixed * (1.0 - fraction) + thick_full[...] * share, mixed)
            parts.append(convected)
        weight = jnp.take_along_axis(
            weights[...], jnp.full((LEV, 128), row, I32), axis=1, mode="promise_in_bounds"
        )
        turned = [pltpu.roll(part, 127, 1) for part in parts]
        between = parts[0] + weight * (jnp.where(lane == 127, turned[1], turned[0]) - parts[0])
        out_ref[r, :, 0:128] = between
        out_ref[r, :, 128:256] = parts[1] + weight * (jnp.where(lane == 127, 0.0, turned[1]) - parts[1])
        sent = jnp.where(lane == 127, weight * turned[0], between)
        edge[row] = jnp.where(low_lane, sent[0:64, :], pltpu.roll(sent[64:128, :], PACK, 1)).astype(BF16)

    def rows_of(pair, carry):
        for i in range(UNROLL):
            one_row(pair * UNROLL + i)
        halo_copy(step * 2 + pair).start()
        return carry

    lax.fori_loop(0, 8 // UNROLL, rows_of, 0)

    @pl.when((step == 0) & has_north)
    def _():
        first[...] = out_ref[0]
        next_copy(1).start()
        next_copy(2).start()

    @pl.when(step == 3)
    def _():
        @pl.when(has_north)
        def _():
            for which in range(3):
                next_copy(which).wait_send()

        @pl.when(has_south)
        def _():
            for which in range(3):
                next_copy(which).wait_recv()

        for block in range(ROWS // 4):
            halo_copy(block).wait()


def column_step(rows, meta, field, mixing, top, frac, thick, courant, shift, zfrac):
    whole = lambda *shape: pl.BlockSpec(shape, lambda i: (0,) * len(shape))
    anywhere = pl.BlockSpec(memory_space=pl.ANY)
    return pl.pallas_call(
        column_kernel,
        grid=(4,),
        out_shape=[
            jax.ShapeDtypeStruct((ROWS, LEV, COLS), F32),
            jax.ShapeDtypeStruct((ROWS, 64, 128), BF16),
            jax.ShapeDtypeStruct((LEV, COLS), F32),
            jax.ShapeDtypeStruct((64, 128), BF16),
            jax.ShapeDtypeStruct((LEV + 8, COLS), F32),
        ],
        in_specs=[
            whole(OBS, LEV),
            whole(NDEV, 128),
            anywhere,
            pl.BlockSpec((8, LEV, LEV), lambda i: (i, 0, 0)),
            whole(ROWS, COLS),
            whole(ROWS, COLS),
            whole(1, LEV),
            anywhere,
            whole(ROWS, LEV),
            whole(ROWS, LEV),
        ],
        out_specs=[pl.BlockSpec((8, LEV, COLS), lambda i: (i, 0, 0))] + [anywhere] * 4,
        scratch_shapes=[
            pltpu.VMEM((LEV, OBS), F32),
            pltpu.VMEM((OBS, COLS), BF16),
            pltpu.VMEM((1, OBS), F32),
            pltpu.VMEM((LEV, 128), F32),
            pltpu.VMEM((8 * LEV, COLS), F32),
            pltpu.VMEM((LEV + 8, COLS), F32),
            pltpu.VMEM((LEV, COLS), F32),
            pltpu.VMEM((ROWS, 64, 128), BF16),
            pltpu.VMEM((ROWS, 2, LEV, 128), F32),
            pltpu.VMEM((ROWS, COLS), F32),
            pltpu.VMEM((LEV, 128), F32),
            DMA((2, ROWS // 4)),
            DMA((2, 3)),
            DMA((4,)),
            DMA((2,)),
        ],
        compiler_params=pltpu.CompilerParams(
            vmem_limit_bytes=56 * 1024 * 1024, collective_id=1, has_side_effects=True
        ),
        name="column",
    )(rows, meta, field.reshape(LEV, 64, 128), mixing, top, frac, thick, courant.reshape(LEV, 64, 128), shift, zfrac)


def place(row, half):
    return row // 8 * 16 + half * 8 + row % 8


def transport_kernel(
    conv_hbm, halo_hbm, next_conv_ref, next_halo_ref, next_given_ref, shift_ref, courant_hbm, out_hbm,
    conv, halo, courant, out, shifts, moved, conv_sems, courant_sems, halo_sems, out_sem,
):
    last = lax.axis_index("lat") == NLAT - 1
    groups = ROWS // GROUP

    def conv_copy(group):
        rows = pl.ds(group * GROUP, GROUP)
        return pltpu.make_async_copy(conv_hbm.at[rows], conv.at[rows], conv_sems.at[group])

    def halo_copy(group):
        rows = pl.ds(group * GROUP, GROUP)
        return pltpu.make_async_copy(halo_hbm.at[rows], halo.at[rows], halo_sems.at[group])

    def fetch(group):
        conv_copy(group).start()
        halo_copy(group).start()
        for i in range(GROUP):
            row = group * GROUP + i
            for half in range(2):
                pltpu.make_async_copy(
                    courant_hbm.at[:, place(row, half), :], courant.at[row, half], courant_sems.at[group]
                ).start()

    for ahead in range(AHEAD):
        fetch(groups - 1 - ahead)

    given = jnp.where(last, 0.0, next_given_ref[128:136, :])
    blank = jnp.zeros((LEV - ROWS - 1, 128), F32)
    by_row = jnp.transpose(
        jnp.concatenate([shift_ref[...].astype(F32), given[0:1, 0:128], blank], axis=0)
    )
    column = iota((LEV, 128), 1)
    ones = jnp.ones((128, 128), BF16)
    for row in range(ROWS + 1):
        alone = jnp.where(column == row, by_row, 0.0).astype(BF16)
        shifts[row, :, :] = jnp.dot(alone, ones, preferred_element_type=F32).astype(I32)
    lane = iota((PART, 128), 1)

    def lanes(values, index):
        return jnp.take_along_axis(values, index, axis=1, mode="promise_in_bounds")

    def zonal(first, second, packed, part, row):
        levels = pl.ds(part * PART, PART)
        third = packed[pl.ds(part * PART % 64, PART), :].astype(F32)
        if part * PART >= 64:
            third = pltpu.roll(third, PACK, 1)
        shift = shifts[row, levels, :]
        second = second + jnp.where(lane == 127, third, 0.0)
        index = lane + shift
        wrapped = index & 127
        a = lanes(jnp.where(lane < shift, third, first), wrapped)
        b = lanes(second, wrapped)
        inside = index < 128
        return jnp.where(inside, a, b), jnp.where(inside, b, a)

    for part in range(LEV // PART):
        levels = pl.ds(part * PART, PART)
        both = zonal(next_conv_ref[levels, 0:128], next_conv_ref[levels, 128:256], next_halo_ref, part, ROWS)
        for half in range(2):
            span = pl.ds(half * 128, 128)
            moved[half, levels, :] = jnp.where(last, 0.0, next_given_ref[levels, span] * both[half])
    def step(back, carry):
        group = groups - 1 - back
        rows = pl.ds(group * GROUP, GROUP)

        @pl.when(group >= AHEAD)
        def _():
            fetch(group - AHEAD)

        conv_copy(group).wait()
        halo_copy(group).wait()
        pltpu.make_async_copy(courant.at[rows], courant.at[rows], courant_sems.at[group]).wait()
        for part in range(LEV // PART):
            levels = pl.ds(part * PART, PART)
            coming = [moved[0, levels, :], moved[1, levels, :]]
            for i in reversed(range(GROUP)):
                row = group * GROUP + i
                both = zonal(conv[row, levels, 0:128], conv[row, levels, 128:256], halo.at[row], part, row)
                for half in range(2):
                    leaving = courant[row, half, levels, :] * both[half]
                    out[row, half, levels, :] = both[half] - leaving + coming[half]
                    coming[half] = leaving
            for half in range(2):
                moved[half, levels, :] = coming[half]
        for i in range(GROUP):
            row = group * GROUP + i
            for half in range(2):
                pltpu.make_async_copy(
                    out.at[row, half], out_hbm.at[:, place(row, half), :], out_sem
                ).start()
        return carry

    lax.fori_loop(0, groups, step, 0)
    pltpu.make_async_copy(out, out, out_sem).wait()


def transport(conv, halo, next_conv, next_halo, next_given, shift, courant):
    vmem = pl.BlockSpec(memory_space=pltpu.VMEM)
    anywhere = pl.BlockSpec(memory_space=pl.ANY)
    return pl.pallas_call(
        transport_kernel,
        out_shape=jax.ShapeDtypeStruct((LEV, 64, 128), F32),
        in_specs=[anywhere, anywhere] + [vmem] * 4 + [anywhere],
        out_specs=anywhere,
        scratch_shapes=[
            pltpu.VMEM((ROWS, LEV, COLS), F32),
            pltpu.VMEM((ROWS, 64, 128), BF16),
            pltpu.VMEM((ROWS, 2, LEV, 128), F32),
            pltpu.VMEM((ROWS, 2, LEV, 128), F32),
            pltpu.VMEM((ROWS + 1, LEV, 128), I32),
            pltpu.VMEM((2, LEV, 128), F32),
            DMA((ROWS // GROUP,)),
            DMA((ROWS // GROUP,)),
            DMA((ROWS // GROUP,)),
            DMA,
        ],
        compiler_params=pltpu.CompilerParams(vmem_limit_bytes=60 * 1024 * 1024),
        name="transport",
    )(conv, halo, next_conv, next_halo, next_given, shift, courant.reshape(LEV, 64, 128))


def tiles(value):
    return value.reshape(LEV, 4, 8, 2, 128).transpose(0, 1, 3, 2, 4).reshape(LEV, 4, 16, 128)


def untiles(value):
    return value.reshape(LEV, 4, 2, 8, 128).transpose(0, 1, 3, 2, 4).reshape(LEV, ROWS, COLS)


def shards(
    adjoint_field, mixing_inverse, cloud_top, conv_frac, thickness, zonal_shift, zonal_frac,
    merid_courant, obs_kernel, obs_depart, obs_dest, obs_col, obs_count,
):
    courant = tiles(merid_courant)
    shift, zfrac = zonal_shift.T, zonal_frac.T
    rows, meta = exchange(obs_count, obs_kernel, obs_depart, obs_dest, obs_col)
    conv, halo, next_conv, next_halo, next_given = column_step(
        rows.reshape(OBS, LEV), meta.reshape(NDEV, 128), tiles(adjoint_field), mixing_inverse,
        cloud_top, conv_frac, thickness.reshape(1, LEV), courant, shift, zfrac,
    )
    out = transport(conv, halo, next_conv, next_halo, next_given, shift, courant)
    return untiles(out)


def solution(mesh):
    split = P(None, "lat", "lon")
    both = P(("lat", "lon"))
    return jax.shard_map(
        shards,
        mesh=mesh,
        in_specs=(
            split, P("lat", None, None), P("lat", "lon"), P("lat", "lon"), P(), P(None, "lat"), P(None, "lat"),
            split, P(("lat", "lon"), None), both, both, both, both,
        ),
        out_specs=split,
        check_vma=False,
    )
```
